128 devices in a mesh: row: 16 (over y, x), col: 8 (over z, core).
Axes of the slice: x: 4, y: 4, z: 4, core: 2. Of those that a mesh axis runs over, the one named last changes fastest.
Arguments:
- x_blocks: bfloat16 [128, 16, 256, 256], P('row', 'col'), may hold values from -0.75 to 0.75, as said below
- x_cols: int32 [128, 16], P('row', 'col'), may hold values from -1 to 127, as said below
- out_cols: int32 [128, 32], P('row', 'col'), may hold values from 0 to 127, as said below
- branch_flag: int32 [128], P('row'), may hold values from 0 to 1
Outputs:
- purified: bfloat16 [128, 32, 256, 256], P('row', 'col')
- trace: float32 [1], replicated
The draws below stay inside these ranges and needn't reach their ends.
Inputs may be any that keep to these rules, and one draw needn't show every extreme that they name: `x_cols`: slot c * 2 + s of block row i holds -1 or a block column in c * 16 to (c + 1) * 16 - 1; the filled columns of one block row are distinct. The pattern is symmetric: block row i names column j exactly when block row j names column i. The rows of one device hold at most 13 filled slots together, and the rows of some device hold exactly 13. `x_blocks`: the stored block of position (j, i) is the transpose of the stored block of position (i, j); stored diagonal blocks are symmetric. `out_cols`: slot c * 4 + o of block row i holds a block column in c * 16 to (c + 1) * 16 - 1, distinct within one block row; column i is always among the slots of block row i. `branch_flag`: entry i is 0 where block row i takes X times X, 1 where it takes 2 X minus X times X.
All inputs are finite; a program needn't handle non-finite values.
Results may differ from the reference program's by a relative error of at most 0.001.
Values may be sent and summed in bfloat16 or wider, within the bound.
A program may use at most 192 MiB of HBM per device.

```python
import jax
import jax.numpy as jnp
from jax import lax

BLOCK = 256
ROW_BLOCKS = 8
SLOTS = 2
OUT_SLOTS = 4
BLOCKS = 128
COL_BLOCKS = 16
PACKED = 13


def device_perms(key, devs, length):
    return jax.vmap(lambda sub: jax.random.permutation(sub, length))(jax.random.split(key, devs))


def fill_pattern(key):
    n_col = BLOCKS // COL_BLOCKS
    n_row = BLOCKS // ROW_BLOCKS
    ratio = n_row // n_col
    key = jax.random.fold_in(key, 11)
    keys = jax.random.split(key, 6)
    heavy_cap = (PACKED + 1) // 2
    light_cap = PACKED // 2
    devices = jnp.arange(n_row, dtype=jnp.int32)
    dev_first = devices[:, None]
    dev_second = devices[None, :]
    square_caps = jnp.where((dev_first + dev_second) % 2 == 0, heavy_cap, light_cap).astype(jnp.int32)
    low_counts = (square_caps + 1) // 2
    raw_counts = jax.random.randint(keys[0], (n_row, n_row), low_counts, square_caps + 1)
    counts = jnp.where(dev_first <= dev_second, raw_counts, raw_counts.T)
    forced_row = jax.random.randint(keys[1], (), 0, n_row)
    forced_col = jax.random.randint(keys[2], (), 0, n_col)
    forced_hit = (dev_first == forced_row) & (dev_second // ratio == forced_col) | (dev_second == forced_row) & (dev_first // ratio == forced_col)
    counts = jnp.where(forced_hit, square_caps, counts)
    local = jnp.arange(ROW_BLOCKS, dtype=jnp.int32)
    squares = n_row * n_row
    column_perm = device_perms(keys[3], squares, ROW_BLOCKS).reshape(n_row, n_row, ROW_BLOCKS)
    keep_rank = device_perms(keys[4], squares, ROW_BLOCKS).reshape(n_row, n_row, ROW_BLOCKS)
    keep = keep_rank < counts[:, :, None]
    loose = ((column_perm[..., None] == local) & keep[..., None]).astype(jnp.int32)
    match_perm = device_perms(keys[5], n_row, ROW_BLOCKS)
    diag_counts = jnp.diagonal(counts)
    paired_limit = 2 * (diag_counts // 2)
    partner_spot = jnp.where(local[None, :] < paired_limit[:, None], jnp.bitwise_xor(local, 1)[None, :], local[None, :])
    active = (local[None, :] < diag_counts[:, None]).astype(jnp.int32)
    row_of = match_perm
    col_of = jnp.take_along_axis(match_perm, partner_spot, axis=1)
    row_hot = (row_of[..., None] == local).astype(jnp.int32) * active[..., None]
    col_hot = (col_of[..., None] == local).astype(jnp.int32)
    sym = jnp.sum(row_hot[:, :, :, None] * col_hot[:, :, None, :], axis=1)
    mirrored = jnp.swapaxes(jnp.swapaxes(loose, 0, 1), 2, 3)
    diag_part = jnp.broadcast_to(sym[:, None], (n_row, n_row, ROW_BLOCKS, ROW_BLOCKS))
    upper = (dev_first < dev_second)[..., None, None]
    lower = (dev_first > dev_second)[..., None, None]
    adj = jnp.where(upper, loose, jnp.where(lower, mirrored, diag_part))
    full = adj.transpose(0, 2, 1, 3).reshape(BLOCKS, BLOCKS)
    grouped = full.reshape(BLOCKS, n_col, COL_BLOCKS)
    rank = jnp.cumsum(grouped, axis=2) - 1
    totals = jnp.sum(grouped, axis=2)
    group_spots = jnp.arange(COL_BLOCKS, dtype=jnp.int32)
    group_base = (jnp.arange(n_col, dtype=jnp.int32) * COL_BLOCKS)[None, :]
    slot_list = []
    for slot in range(SLOTS):
        chosen = (grouped > 0) & (rank == slot)
        where_col = jnp.sum(jnp.where(chosen, group_spots[None, None, :], 0), axis=2)
        slot_list.append(jnp.where(totals > slot, group_base + where_col, -1))
    columns = jnp.stack(slot_list, axis=2)
    return columns.reshape(BLOCKS, n_col * SLOTS).astype(jnp.int32)


def draw_x_cols(key, part):
    return fill_pattern(key)


def draw_x_blocks(key, part):
    columns = fill_pattern(key)
    width = columns.shape[1]
    live = columns >= 0
    safe = jnp.where(live, columns, 0)
    rows_there = columns[safe]
    own_rows = jnp.arange(BLOCKS, dtype=jnp.int32)[:, None, None]
    back = jnp.sum(jnp.where(rows_there == own_rows, jnp.arange(width, dtype=jnp.int32)[None, None, :], 0), axis=2)
    flat_self = jnp.arange(BLOCKS, dtype=jnp.int32)[:, None] * width + jnp.arange(width, dtype=jnp.int32)[None, :]
    mirror = jnp.where(live, safe * width + back, flat_self).reshape(-1)
    key_vals = jax.random.fold_in(key, 31)
    shape = (BLOCKS * width, BLOCK, BLOCK)
    raw = jax.random.truncated_normal(key_vals, -4.0, 4.0, shape, jnp.float32) * 0.125
    values = (raw + jnp.swapaxes(raw[mirror], 1, 2)) * 0.7071067811865476
    return values.reshape(BLOCKS, width, BLOCK, BLOCK).astype(jnp.bfloat16)


def draw_out_cols(key, part):
    n_col = BLOCKS // COL_BLOCKS
    columns = fill_pattern(key)
    every = jnp.arange(BLOCKS)
    present = jnp.sum((columns[:, :, None] == every[None, None, :]).astype(jnp.int32), axis=1)
    present = jnp.minimum(present, 1)
    second = jnp.dot(present, present)
    eye = (every[:, None] == every[None, :]).astype(jnp.int32)
    reach = jnp.minimum(second + present + eye, 1).reshape(BLOCKS, n_col, COL_BLOCKS)
    diag = eye.reshape(BLOCKS, n_col, COL_BLOCKS)
    key_rank = jax.random.fold_in(key, 23)
    ranks = jax.vmap(lambda k: jax.random.permutation(k, COL_BLOCKS))(jax.random.split(key_rank, BLOCKS * n_col))
    ranks = ranks.reshape(BLOCKS, n_col, COL_BLOCKS)
    scores = diag * 4 * (COL_BLOCKS + 1) + reach * (COL_BLOCKS + 1) + ranks
    best = jax.lax.top_k(scores, OUT_SLOTS)[1]
    best = best + (jnp.arange(n_col) * COL_BLOCKS)[None, :, None]
    return best.reshape(BLOCKS, n_col * OUT_SLOTS).astype(jnp.int32)


def touch_ends(values, own_key, low, high):
    place = [jax.random.randint(jax.random.fold_in(own_key, axis), (), 0, length) for axis, length in enumerate(values.shape)]
    widest = values.shape.index(max(values.shape))
    next_to = place[:widest] + [(place[widest] + 1) % values.shape[widest]] + place[widest + 1:]
    return values.at[tuple(place)].set(low).at[tuple(next_to)].set(high)


def setup_inputs(seed: int = 0) -> dict:
    splits = jax.random.split(jax.random.key(seed), 5)
    x_blocks = draw_x_blocks(jax.random.fold_in(splits[4], 71), 0)
    x_cols = draw_x_cols(jax.random.fold_in(splits[4], 71), 0)
    out_cols = draw_out_cols(jax.random.fold_in(splits[4], 71), 0)
    branch_flag = touch_ends(jax.random.randint(splits[3], (BLOCKS,), 0, 2), jax.random.fold_in(splits[3], 1), 0, 1).astype(jnp.int32)
    return {"x_blocks": x_blocks, "x_cols": x_cols, "out_cols": out_cols, "branch_flag": branch_flag}


def reference(x_blocks, x_cols, out_cols, branch_flag):
    n_col = x_cols.shape[1] // SLOTS
    filled = x_cols >= 0
    cleared = jnp.where(filled[:, :, None, None], x_blocks, jnp.zeros_like(x_blocks))

    def one_row(index):
        flag_on = branch_flag[index] == 1
        cols = x_cols[index]
        live = cols >= 0
        source = jnp.where(live, cols, 0).astype(jnp.int32)
        lhs = cleared[index].astype(jnp.float32)
        fetched_all = cleared[source]
        fetched_cols_all = jnp.where(live[:, None], x_cols[source], -1)
        targets = out_cols[index]

        def by_device(device):
            start = (device * SLOTS).astype(jnp.int32)
            ostart = (device * OUT_SLOTS).astype(jnp.int32)
            fetched = lax.dynamic_slice_in_dim(fetched_all, start, SLOTS, 1).astype(jnp.float32)
            fetched_cols = lax.dynamic_slice_in_dim(fetched_cols_all, start, SLOTS, 1)
            chosen = lax.dynamic_slice_in_dim(targets, ostart, OUT_SLOTS, 0)
            products = jnp.einsum("exy,esyz->esxz", lhs, fetched, precision=lax.Precision.HIGHEST)
            match = (fetched_cols[None, :, :] == chosen[:, None, None]).astype(jnp.float32)
            square = jnp.einsum("oes,esxz->oxz", match, products, precision=lax.Precision.HIGHEST)
            own_cols = lax.dynamic_slice_in_dim(cols, start, SLOTS, 0)
            own_match = (own_cols[None, :] == chosen[:, None]).astype(jnp.float32)
            own_blocks = lax.dynamic_slice_in_dim(cleared[index], start, SLOTS, 0).astype(jnp.float32)
            own = jnp.einsum("os,sxz->oxz", own_match, own_blocks, precision=lax.Precision.HIGHEST)
            return square, own

        square, own = lax.map(by_device, jnp.arange(n_col, dtype=jnp.int32))
        square = square.reshape(n_col * OUT_SLOTS, BLOCK, BLOCK)
        own = own.reshape(n_col * OUT_SLOTS, BLOCK, BLOCK)
        result = jnp.where(flag_on, 2.0 * own - square, square)
        diag_here = (targets == index).astype(jnp.float32)
        part = jnp.sum(diag_here * jnp.trace(result, axis1=1, axis2=2))
        return result.astype(jnp.bfloat16), part

    purified, parts = lax.map(one_row, jnp.arange(BLOCKS, dtype=jnp.int32))
    trace = jnp.sum(parts).reshape(1)
    return purified, trace
```

```python
import jax
import jax.numpy as jnp
from jax import lax
from jax.experimental import pallas as pl
from jax.experimental.pallas import tpu as pltpu
from jax.sharding import PartitionSpec as P

MESH = pl.DeviceIdType.MESH
BLK = 256
ROWS = 8
SLOTS = 2
KEPT = 4
PACKED = 13
TILE = PACKED * BLK
CUT = TILE // 4
RING = 4
SPAN = 16
LANES = 128
TRACE_LANE = 32
LOOKAHEAD = 1.0


def build_plan():
    items = {}
    step = {"x+": (1, 0), "x-": (-1, 0), "y+": (0, 1), "y-": (0, -1)}

    for q in range(4):
        first, second = ("x", "y") if q < 2 else ("y", "x")
        arrived = {(0, 0): None}

        def send(link, off):
            key = ("B", link, off[0] % RING, off[1] % RING, q)
            pre = arrived[(off[0] % RING, off[1] % RING)]
            items[key] = dict(link=link, size=1.0, pre=[pre] if pre else [])
            move = step[link]
            arrived[((off[0] - move[0]) % RING, (off[1] - move[1]) % RING)] = key

        def line(axis, base):
            unit = (1, 0) if axis == "x" else (0, 1)
            send(axis + "+", base)
            send(axis + "-", base)
            if q % 2 == 0:
                send(axis + "+", (base[0] - unit[0], base[1] - unit[1]))
            else:
                send(axis + "-", (base[0] + unit[0], base[1] + unit[1]))

        line(first, (0, 0))
        for off in range(RING):
            line(second, (off, 0) if first == "x" else (0, off))

    for q in range(4):
        items[("A", "z+", 0, q)] = dict(link="z+", size=1.0, pre=[])
        items[("A", "z-", 0, q)] = dict(link="z-", size=1.0, pre=[])
        if q % 2 == 0:
            items[("A", "z+", 3, q)] = dict(link="z+", size=1.0, pre=[("A", "z+", 0, q)])
            far = ("A", "z+", 3, q)
        else:
            items[("A", "z-", 1, q)] = dict(link="z-", size=1.0, pre=[("A", "z-", 0, q)])
            far = ("A", "z-", 1, q)
        items[("A", "s", 0, q)] = dict(link="s", size=0.2, pre=[])
        items[("A", "s", 3, q)] = dict(link="s", size=0.2, pre=[("A", "z+", 0, q)])
        items[("A", "s", 1, q)] = dict(link="s", size=0.2, pre=[("A", "z-", 0, q)])
        items[("A", "s", 2, q)] = dict(link="s", size=0.2, pre=[far])

    before = []
    for axis in "xyz":
        items[("M", axis + "+", 0)] = dict(link=axis + "+", size=0.02, pre=list(before))
        items[("M", axis + "-", 0)] = dict(link=axis + "-", size=0.02, pre=list(before))
        items[("M", axis + "+", 3)] = dict(link=axis + "+", size=0.02, pre=[("M", axis + "+", 0)])
        before = before + [("M", axis + "+", 0), ("M", axis + "-", 0), ("M", axis + "+", 3)]
    items[("M", "s", 0)] = dict(link="s", size=0.02, pre=list(before))

    after = {key: [] for key in items}
    for key, item in items.items():
        for pre in item["pre"]:
            after[pre].append(key)
    rank = {}

    def depth(key):
        if key not in rank:
            rank[key] = items[key]["size"] + max([depth(k) for k in after[key]] or [0.0])
        return rank[key]

    latency = 0.2
    free = {item["link"]: 0.0 for item in items.values()}
    start, landed = {}, {}
    todo = list(items)
    while todo:
        best = None
        for key in todo:
            if any(pre not in landed for pre in items[key]["pre"]):
                continue
            ready = max([landed[pre] for pre in items[key]["pre"]] or [0.0])
            at = max(ready, free[items[key]["link"]])
            small = 0 if key[0] == "M" else 1
            mark = (at, small, -depth(key))
            if best is None or mark < best[0]:
                best = (mark, key, ready, at)
        _, key, ready, at = best
        todo.remove(key)
        start[key] = (max(ready, at - LOOKAHEAD), at, len(start))
        free[items[key]["link"]] = at + items[key]["size"]
        landed[key] = at + items[key]["size"] + latency
    order = sorted(items, key=lambda key: start[key])
    return order, items, max(landed.values())


ORDER, ITEMS, PLAN_SLOTS = build_plan()
NUMBER = {key: index for index, key in enumerate(ORDER)}


def place():
    row = lax.axis_index("row")
    col = lax.axis_index("col")
    return lax.rem(row, RING), row // RING, col // 2, lax.rem(col, 2)


def turn(value, by):
    return lax.rem(value + by % RING, RING)


def pack_kernel(cols, flags, x_ref, ga, gb, meta, buf, source, line, acc, in_sem, out_sem):
    row = lax.axis_index("row")
    col = lax.axis_index("col")
    x, y, z, core = place()
    for t in range(PACKED):
        source[t] = 0
    lane = lax.broadcasted_iota(jnp.int32, (1, LANES), 1)
    count = jnp.int32(0)
    info = jnp.zeros((1, LANES), jnp.float32)
    for s in range(ROWS * SLOTS):
        entry = cols[s // SLOTS, s % SLOTS]
        live = entry >= 0

        @pl.when(live)
        def _(s=s, count=count):
            source[count] = s

        info = jnp.where(lane == s, entry.astype(jnp.float32), info)
        info = jnp.where(lane == 16 + s, count.astype(jnp.float32), info)
        count = count + live.astype(jnp.int32)

    def fetch(t):
        s = source[t]
        return pltpu.make_async_copy(
            x_ref.at[s // SLOTS, lax.rem(s, SLOTS)], buf.at[pl.ds(t * BLK, BLK)], in_sem.at[t]
        )

    for t in range(PACKED):
        fetch(t).start()
    for t in range(PACKED):
        fetch(t).wait()
    outs = [
        pltpu.make_async_copy(buf, gb.at[row], out_sem.at[0]),
        pltpu.make_async_copy(buf, ga.at[col], out_sem.at[1]),
    ]
    for copy in outs:
        copy.start()

    acc[...] = jnp.zeros_like(acc)
    diag = lax.broadcasted_iota(jnp.int32, (BLK, BLK), 0) == lax.broadcasted_iota(
        jnp.int32, (BLK, BLK), 1
    )

    def term(t, carry):
        s = source[t]
        local = s // SLOTS
        flag = flags[local] == 1
        weight = jnp.where(flag, -1.0, 1.0).astype(jnp.float32)
        block = buf[pl.ds(pl.multiple_of(t * BLK, BLK), BLK), :].astype(jnp.float32)
        acc[...] += weight * jnp.sum((block * block).reshape(BLK // 8, 8, BLK), axis=0)

        @pl.when(flag & (cols[local, lax.rem(s, SLOTS)] == row * ROWS + local))
        def _():
            kept = jnp.where(diag, block, 0.0)
            acc[...] += 2.0 * jnp.sum(kept.reshape(BLK // 8, 8, BLK), axis=0)

        return carry

    lax.fori_loop(0, count, term, 0)
    line[...] = jnp.where(lane == TRACE_LANE, jnp.sum(acc[...]), info)
    last = pltpu.make_async_copy(line, meta.at[core * 64 + z * 16 + y * 4 + x], out_sem.at[2])
    last.start()
    for copy in outs + [last]:
        copy.wait()


def gather_kernel(ga_in, gb_in, meta_in, ga, gb, meta, send_sem, recv_sem):
    x, y, z, core = place()

    def peer(link):
        by = 1 if link.endswith("+") else -1
        if link[0] == "x":
            return {"row": y * RING + turn(x, by), "col": z * 2 + core}
        if link[0] == "y":
            return {"row": turn(y, by) * RING + x, "col": z * 2 + core}
        if link[0] == "z":
            return {"row": y * RING + x, "col": turn(z, by) * 2 + core}
        return {"row": y * RING + x, "col": z * 2 + 1 - core}

    def region(key, at):
        px, py, pz, pcore = at
        if key[0] == "B":
            slot = turn(py, key[3]) * RING + turn(px, key[2])
            return gb.at[slot, pl.ds(key[4] * CUT, CUT)]
        if key[0] == "A":
            slot = turn(pz, key[2]) * 2 + pcore
            return ga.at[slot, pl.ds(key[3] * CUT, CUT)]
        axis = key[1][0]
        if axis == "x":
            return meta.at[pl.ds(pcore * 64 + pz * 16 + py * 4 + turn(px, key[2]), 1)]
        if axis == "y":
            return meta.at[pl.ds(pcore * 64 + pz * 16 + turn(py, key[2]) * 4, 4)]
        if axis == "z":
            return meta.at[pl.ds(pcore * 64 + turn(pz, key[2]) * 16, 16)]
        return meta.at[pl.ds(pcore * 64, 64)]

    def outgoing(key):
        piece = region(key, (x, y, z, core))
        n = NUMBER[key]
        return pltpu.make_async_remote_copy(
            src_ref=piece,
            dst_ref=piece,
            send_sem=send_sem.at[n],
            recv_sem=recv_sem.at[n],
            device_id=peer(key[1]),
            device_id_type=MESH,
        )

    def incoming(key):
        link = key[1]
        by = -1 if link.endswith("+") else 1
        at = (x, y, z, core)
        if link[0] == "x":
            at = (turn(x, by), y, z, core)
        elif link[0] == "y":
            at = (x, turn(y, by), z, core)
        elif link[0] == "z":
            at = (x, y, turn(z, by), core)
        else:
            at = (x, y, z, 1 - core)
        piece = region(key, at)
        n = NUMBER[key]
        return pltpu.make_async_remote_copy(
            src_ref=piece,
            dst_ref=piece,
            send_sem=send_sem.at[n],
            recv_sem=recv_sem.at[n],
            device_id=peer(link),
            device_id_type=MESH,
        )

    barrier = pltpu.get_barrier_semaphore()
    links = ("x+", "x-", "y+", "y-", "z+", "z-", "s")
    for link in links:
        pl.semaphore_signal(barrier, inc=1, device_id=peer(link), device_id_type=MESH)
    pl.semaphore_wait(barrier, len(links))

    seen = set()
    for key in ORDER:
        for pre in ITEMS[key]["pre"]:
            if pre not in seen:
                incoming(pre).wait_recv()
                seen.add(pre)
        outgoing(key).start()
    for key in ORDER:
        if key not in seen:
            incoming(key).wait_recv()
    for key in ORDER:
        outgoing(key).wait_send()


def product_kernel(
    meta, kept, cols, flags, meta_v, x_ref, ga, gb,
    out_ref, trace_ref,
    abuf, bbuf, acc, inv, list_a, list_p, counts, sem,
):
    i = pl.program_id(0)
    x, y, z, core = place()
    row = y * RING + x
    base = (z * 2 + core) * SPAN

    def number(m, at):
        return meta[m, 0, at].astype(jnp.int32)

    def copy_a(slot, n, tile, pos):
        return pltpu.make_async_copy(
            ga.at[tile, pl.ds(pl.multiple_of(pos * BLK, BLK), BLK)], abuf.at[slot, n], sem.at[slot]
        )

    def copy_b(slot, n, tile, pos):
        return pltpu.make_async_copy(
            gb.at[tile, pl.ds(pl.multiple_of(pos * BLK, BLK), BLK)], bbuf.at[slot, n], sem.at[slot]
        )

    def prepare(local, slot):
        for t in range(SPAN):
            inv[t] = -1
        for p in range(KEPT):
            inv[kept[local, p] - base] = p

        def entry(e, carry):
            na, nb = carry
            tile = e // SLOTS
            m = lax.rem(tile, 2) * 64 + tile // 2 * 16 + row
            at = local * SLOTS + lax.rem(e, SLOTS)
            k = number(m, at)

            def live():
                other = k // ROWS
                mb = core * 64 + z * 16 + other
                found = nb
                for s in range(SLOTS):
                    spot = lax.rem(k, ROWS) * SLOTS + s
                    j = number(mb, spot)
                    p = jnp.where(j >= 0, inv[jnp.maximum(j - base, 0)], -1)
                    hit = p >= 0

                    @pl.when(hit)
                    def _(found=found, p=p, spot=spot):
                        list_a[slot, found] = na
                        list_p[slot, found] = p
                        copy_b(slot, found, other, number(mb, 16 + spot)).start()

                    found = found + hit.astype(jnp.int32)

                @pl.when(found > nb)
                def _():
                    copy_a(slot, na, tile, number(m, 16 + at)).start()

                return na + (found > nb).astype(jnp.int32), found

            return lax.cond(k >= 0, live, lambda: (na, nb))

        na, nb = lax.fori_loop(0, 16, entry, (jnp.int32(0), jnp.int32(0)))
        counts[slot, 0] = na
        counts[slot, 1] = nb

    slot = lax.rem(i, 2)

    @pl.when(i == 0)
    def _():
        prepare(0, 0)
        lane = lax.broadcasted_iota(jnp.int32, (128, 1, LANES), 2)
        trace_ref[0, 0] = jnp.sum(jnp.where(lane == TRACE_LANE, meta_v[...], 0.0))

    @pl.when(i + 1 < ROWS)
    def _():
        prepare(i + 1, 1 - slot)

    na, nb = counts[slot, 0], counts[slot, 1]

    def drain(_, carry):
        copy_a(slot, 0, 0, 0).wait()
        return carry

    lax.fori_loop(0, na + nb, drain, 0)
    acc[...] = jnp.zeros_like(acc)

    def product(n, carry):
        p = list_p[slot, n]
        acc[p] += jnp.dot(
            abuf[slot, list_a[slot, n]], bbuf[slot, n], preferred_element_type=jnp.float32
        )
        return carry

    lax.fori_loop(0, nb, product, 0)
    flag = flags[i] == 1
    sign = jnp.where(flag, -1.0, 1.0).astype(jnp.float32)
    for p in range(KEPT):
        j = kept[i, p]
        second = cols[i, 1] == j
        there = second | (cols[i, 0] == j)
        scale = jnp.where(flag & there, 2.0, 0.0).astype(jnp.float32)
        own = x_ref[0, second.astype(jnp.int32)].astype(jnp.float32)
        out_ref[0, p] = (scale * own + sign * acc[p]).astype(jnp.bfloat16)


def per_device(x_blocks, x_cols, out_cols, branch_flag):
    anywhere = pl.BlockSpec(memory_space=pl.ANY)
    scalars = pl.BlockSpec(memory_space=pltpu.SMEM)
    shapes = (
        jax.ShapeDtypeStruct((8, TILE, BLK), jnp.bfloat16),
        jax.ShapeDtypeStruct((16, TILE, BLK), jnp.bfloat16),
        jax.ShapeDtypeStruct((128, 1, LANES), jnp.float32),
    )
    ga, gb, meta = pl.pallas_call(
        pack_kernel,
        name="pack",
        out_shape=shapes,
        in_specs=[scalars, scalars, anywhere],
        out_specs=[anywhere] * 3,
        scratch_shapes=[
            pltpu.VMEM((TILE, BLK), jnp.bfloat16),
            pltpu.SMEM((16,), jnp.int32),
            pltpu.VMEM((1, LANES), jnp.float32),
            pltpu.VMEM((8, BLK), jnp.float32),
            pltpu.SemaphoreType.DMA((PACKED,)),
            pltpu.SemaphoreType.DMA((3,)),
        ],
    )(x_cols, branch_flag, x_blocks)
    ga, gb, meta = pl.pallas_call(
        gather_kernel,
        name="gather",
        out_shape=shapes,
        in_specs=[anywhere] * 3,
        out_specs=[anywhere] * 3,
        scratch_shapes=[
            pltpu.SemaphoreType.DMA((len(ORDER),)),
            pltpu.SemaphoreType.DMA((len(ORDER),)),
        ],
        input_output_aliases={0: 0, 1: 1, 2: 2},
        compiler_params=pltpu.CompilerParams(collective_id=0, has_side_effects=True),
    )(ga, gb, meta)
    purified, trace = pl.pallas_call(
        product_kernel,
        name="product",
        grid=(ROWS,),
        out_shape=(
            jax.ShapeDtypeStruct((ROWS, KEPT, BLK, BLK), jnp.bfloat16),
            jax.ShapeDtypeStruct((1, 1), jnp.float32),
        ),
        in_specs=[
            scalars, scalars, scalars, scalars,
            pl.BlockSpec((128, 1, LANES), lambda i: (0, 0, 0)),
            pl.BlockSpec((1, SLOTS, BLK, BLK), lambda i: (i, 0, 0, 0)),
            anywhere, anywhere,
        ],
        out_specs=[pl.BlockSpec((1, KEPT, BLK, BLK), lambda i: (i, 0, 0, 0)), scalars],
        scratch_shapes=[
            pltpu.VMEM((2, 16, BLK, BLK), jnp.bfloat16),
            pltpu.VMEM((2, 32, BLK, BLK), jnp.bfloat16),
            pltpu.VMEM((KEPT, BLK, BLK), jnp.float32),
            pltpu.SMEM((SPAN,), jnp.int32),
            pltpu.SMEM((2, 32), jnp.int32),
            pltpu.SMEM((2, 32), jnp.int32),
            pltpu.SMEM((2, 2), jnp.int32),
            pltpu.SemaphoreType.DMA((2,)),
        ],
    )(meta, out_cols, x_cols, branch_flag, meta, x_blocks, ga, gb)
    return purified, trace.reshape(1)


def solution(mesh):
    in_specs = (P("row", "col", None, None), P("row", "col"), P("row", "col"), P("row"))
    out_specs = (P("row", "col", None, None), P())
    return jax.shard_map(
        per_device, mesh=mesh, in_specs=in_specs, out_specs=out_specs, check_vma=False
    )
```

```python
import jax
import jax.numpy as jnp
from jax import lax
from jax.experimental import pallas as pl
from jax.experimental.pallas import tpu as pltpu
from jax.sharding import PartitionSpec as P

MESH = pl.DeviceIdType.MESH
BLK = 256
ROWS = 8
SLOTS = 2
KEPT = 4
PACKED = 13
PART = 64
PER = BLK // PART
TILE = PACKED * PER
CUT = TILE // 4
RING = 4
SPAN = 16
LANES = 128
LOOKAHEAD = 1.0


def build_plan():
    items = {}
    step = {"x+": (1, 0), "x-": (-1, 0), "y+": (0, 1), "y-": (0, -1)}

    for q in range(4):
        first, second = ("x", "y") if q < 2 else ("y", "x")
        arrived = {(0, 0): None}

        def send(link, off):
            key = ("B", link, off[0] % RING, off[1] % RING, q)
            pre = arrived[(off[0] % RING, off[1] % RING)]
            items[key] = dict(link=link, size=1.0, pre=[pre] if pre else [])
            move = step[link]
            arrived[((off[0] - move[0]) % RING, (off[1] - move[1]) % RING)] = key

        def line(axis, base):
            unit = (1, 0) if axis == "x" else (0, 1)
            send(axis + "+", base)
            send(axis + "-", base)
            if q % 2 == 0:
                send(axis + "+", (base[0] - unit[0], base[1] - unit[1]))
            else:
                send(axis + "-", (base[0] + unit[0], base[1] + unit[1]))

        line(first, (0, 0))
        for off in range(RING):
            line(second, (off, 0) if first == "x" else (0, off))

    for q in range(4):
        items[("A", "z+", 0, q)] = dict(link="z+", size=1.0, pre=[])
        items[("A", "z-", 0, q)] = dict(link="z-", size=1.0, pre=[])
        if q % 2 == 0:
            items[("A", "z+", 3, q)] = dict(link="z+", size=1.0, pre=[("A", "z+", 0, q)])
            far = ("A", "z+", 3, q)
        else:
            items[("A", "z-", 1, q)] = dict(link="z-", size=1.0, pre=[("A", "z-", 0, q)])
            far = ("A", "z-", 1, q)
        items[("A", "s", 0, q)] = dict(link="s", size=0.2, pre=[])
        items[("A", "s", 3, q)] = dict(link="s", size=0.2, pre=[("A", "z+", 0, q)])
        items[("A", "s", 1, q)] = dict(link="s", size=0.2, pre=[("A", "z-", 0, q)])
        items[("A", "s", 2, q)] = dict(link="s", size=0.2, pre=[far])

    before = []
    for axis in "xyz":
        items[("M", axis + "+", 0)] = dict(link=axis + "+", size=0.02, pre=list(before))
        items[("M", axis + "-", 0)] = dict(link=axis + "-", size=0.02, pre=list(before))
        items[("M", axis + "+", 3)] = dict(link=axis + "+", size=0.02, pre=[("M", axis + "+", 0)])
        before = before + [("M", axis + "+", 0), ("M", axis + "-", 0), ("M", axis + "+", 3)]
    items[("M", "s", 0)] = dict(link="s", size=0.02, pre=list(before))

    source = {}
    for key in items:
        if key[0] == "B":
            move = step[key[1]]
            source[((key[2] - move[0]) % RING, (key[3] - move[1]) % RING, key[4])] = key

    def group(dx, dy):
        return 2 * LINE_ORDER.index(dy) + (1 if dx == 2 else 0)

    due = {key: float(PAIRS * 2) for key in items}
    for (dx, dy, q), key in source.items():
        due[key] = DEADLINES[group(dx, dy)]
    after = {key: [] for key in items}
    for key, item in items.items():
        for pre in item["pre"]:
            after[pre].append(key)
    rank = {}

    def urgency(key):
        if key not in rank:
            rank[key] = min(
                [due[key]] + [urgency(k) - items[k]["size"] - SLACK for k in after[key]]
            )
        return rank[key]

    free = {item["link"]: 0.0 for item in items.values()}
    start, landed = {}, {}
    todo = list(items)
    while todo:
        best = None
        for key in todo:
            if any(pre not in landed for pre in items[key]["pre"]):
                continue
            ready = max([landed[pre] + SLACK for pre in items[key]["pre"]] or [0.0])
            at = max(ready, free[items[key]["link"]])
            small = 0 if key[0] == "M" else 1
            mark = (at, small, urgency(key))
            if best is None or mark < best[0]:
                best = (mark, key, ready, at)
        _, key, ready, at = best
        todo.remove(key)
        start[key] = (max(ready, at - LOOKAHEAD), at, len(start))
        free[items[key]["link"]] = at + items[key]["size"]
        landed[key] = at + items[key]["size"]
    events = [(start[key], ("send", key)) for key in items]

    clock = max(landed[key] for key in items if key[0] == "A") + 0.2
    events.append(((clock, 0.0, 0), ("rows", None)))
    needs = []
    for n in range(PAIRS - LEFT):
        need = [key for (dx, dy, q), key in source.items() if group(dx, dy) <= n
                and group(dx, dy) // 2 == n // 2]
        needs.append(need)
        there = max([landed[key] for key in need]) + 0.2
        began = max(clock - (0.4 if n else 0.0), there)
        events.append(((began, 0.5, n), ("load", n)))
        clock = max(clock, began + 0.3)
        for i in range(0, ROWS, GROUP):
            events.append(((clock, 1.0, i), ("work", (n, i))))
            clock = clock + CHUNK * GROUP
    events.sort()
    order = sorted(items, key=lambda key: start[key])
    return [event for _, event in events], order, items, needs, max(landed.values()), clock


PAIRS = 8
LEFT = 1
LINE_ORDER = (0, 1, 3, 2)
DEADLINES = (2.0, 3.0, 6.0, 7.0, 10.0, 11.0, 14.0, 15.0)
SLACK = 1.0
CHUNK = 0.13
GROUP = 4
EVENTS, ORDER, ITEMS, NEEDS, PLAN_SLOTS, PLAN_WORK = build_plan()
NUMBER = {key: index for index, key in enumerate(ORDER)}


def place():
    row = lax.axis_index("row")
    col = lax.axis_index("col")
    return lax.rem(row, RING), row // RING, col // 2, lax.rem(col, 2)


def turn(value, by):
    return lax.rem(value + by % RING, RING)


def pack_kernel(
    cols, flags, x_ref, ga, gb, meta, share, buf, source, line, total, acc, in_sem, out_sem
):
    row = lax.axis_index("row")
    col = lax.axis_index("col")
    x, y, z, core = place()
    for t in range(PACKED):
        source[t] = 0
    lane = lax.broadcasted_iota(jnp.int32, (1, LANES), 1)
    count = jnp.int32(0)
    info = jnp.zeros((1, LANES), jnp.int32)
    for s in range(ROWS * SLOTS):
        entry = cols[s // SLOTS, s % SLOTS]
        live = entry >= 0

        @pl.when(live)
        def _(s=s, count=count):
            source[count] = s

        info = jnp.where(lane == s, entry, info)
        info = jnp.where(lane == 16 + s, jnp.where(live, count, 0), info)
        count = count + live.astype(jnp.int32)

    def fetch(t):
        s = source[t]
        return pltpu.make_async_copy(
            x_ref.at[s // SLOTS, lax.rem(s, SLOTS)], buf.at[pl.ds(t * PER, PER)], in_sem.at[t]
        )

    for t in range(PACKED):
        fetch(t).start()
    line[...] = info
    outs = [
        pltpu.make_async_copy(line, meta.at[col], out_sem.at[2]),
        pltpu.make_async_copy(line, meta.at[8 + row], out_sem.at[3]),
    ]
    for copy in outs:
        copy.start()
    for t in range(PACKED):
        fetch(t).wait()
    outs = outs + [
        pltpu.make_async_copy(buf, gb.at[row], out_sem.at[0]),
        pltpu.make_async_copy(buf, ga.at[col], out_sem.at[1]),
    ]
    for copy in outs[2:]:
        copy.start()

    acc[...] = jnp.zeros_like(acc)
    diag = lax.broadcasted_iota(jnp.int32, (BLK, BLK), 0) == lax.broadcasted_iota(
        jnp.int32, (BLK, BLK), 1
    )

    def term(t, carry):
        s = source[t]
        local = s // SLOTS
        flag = flags[local] == 1
        weight = jnp.where(flag, -1.0, 1.0).astype(jnp.float32)
        block = buf[pl.ds(t * PER, PER)].reshape(BLK, BLK).astype(jnp.float32)
        acc[...] += weight * jnp.sum((block * block).reshape(BLK // 8, 8, BLK), axis=0)

        @pl.when(flag & (cols[local, lax.rem(s, SLOTS)] == row * ROWS + local))
        def _():
            kept = jnp.where(diag, block, 0.0)
            acc[...] += 2.0 * jnp.sum(kept.reshape(BLK // 8, 8, BLK), axis=0)

        return carry

    lax.fori_loop(0, count, term, 0)
    total[...] = jnp.where(lane == 0, jnp.sum(acc[...]), 0.0)
    last = pltpu.make_async_copy(
        total, share.at[core * 64 + z * 16 + y * 4 + x], out_sem.at[4]
    )
    last.start()
    for copy in outs + [last]:
        copy.wait()


def gather_kernel(
    kept, ga_in, gb_in, meta_in, share_in, ga, gb, meta, share, part,
    a0, a1, b0, b1, acc, words, send_sem, recv_sem, note_send, note_recv, load_sem, out_sem,
):
    row = lax.axis_index("row")
    col = lax.axis_index("col")
    x, y, z, core = place()

    def peer(link):
        by = 1 if link.endswith("+") else -1
        if link[0] == "x":
            return {"row": y * RING + turn(x, by), "col": z * 2 + core}
        if link[0] == "y":
            return {"row": turn(y, by) * RING + x, "col": z * 2 + core}
        if link[0] == "z":
            return {"row": y * RING + x, "col": turn(z, by) * 2 + core}
        return {"row": y * RING + x, "col": z * 2 + 1 - core}

    def region(key, at):
        px, py, pz, pcore = at
        if key[0] == "B":
            slot = turn(py, key[3]) * RING + turn(px, key[2])
            return gb.at[slot, pl.ds(key[4] * CUT, CUT)]
        if key[0] == "A":
            slot = turn(pz, key[2]) * 2 + pcore
            return ga.at[slot, pl.ds(key[3] * CUT, CUT)]
        axis = key[1][0]
        if axis == "x":
            return share.at[pl.ds(pcore * 64 + pz * 16 + py * 4 + turn(px, key[2]), 1)]
        if axis == "y":
            return share.at[pl.ds(pcore * 64 + pz * 16 + turn(py, key[2]) * 4, 4)]
        if axis == "z":
            return share.at[pl.ds(pcore * 64 + turn(pz, key[2]) * 16, 16)]
        return share.at[pl.ds(pcore * 64, 64)]

    def outgoing(key):
        piece = region(key, (x, y, z, core))
        n = NUMBER[key]
        return pltpu.make_async_remote_copy(
            src_ref=piece,
            dst_ref=piece,
            send_sem=send_sem.at[n],
            recv_sem=recv_sem.at[n],
            device_id=peer(key[1]),
            device_id_type=MESH,
        )

    def incoming(key):
        link = key[1]
        by = -1 if link.endswith("+") else 1
        at = (x, y, z, core)
        if link[0] == "x":
            at = (turn(x, by), y, z, core)
        elif link[0] == "y":
            at = (x, turn(y, by), z, core)
        elif link[0] == "z":
            at = (x, y, turn(z, by), core)
        else:
            at = (x, y, z, 1 - core)
        piece = region(key, at)
        n = NUMBER[key]
        return pltpu.make_async_remote_copy(
            src_ref=piece,
            dst_ref=piece,
            send_sem=send_sem.at[n],
            recv_sem=recv_sem.at[n],
            device_id=peer(link),
            device_id_type=MESH,
        )

    def note_slots(n):
        if n < 7:
            return col, lax.rem(col + 7 - n, 8)
        return 8 + row, 8 + lax.rem(row + 22 - n, 16)

    def note_device(n):
        if n < 7:
            return {"row": row, "col": lax.rem(col + n + 1, 8)}
        return {"row": lax.rem(row + n - 6, 16), "col": col}

    def note(n, slot):
        return pltpu.make_async_remote_copy(
            src_ref=meta.at[slot],
            dst_ref=meta.at[slot],
            send_sem=note_send.at[n],
            recv_sem=note_recv.at[n],
            device_id=note_device(n),
            device_id_type=MESH,
        )

    barrier = pltpu.get_barrier_semaphore()
    for n in range(22):
        pl.semaphore_signal(barrier, inc=1, device_id=note_device(n), device_id_type=MESH)
    zero = jnp.zeros((PART, BLK), jnp.bfloat16)
    for t in range(PER):
        b0[2 * TILE + t] = zero
        b1[2 * TILE + t] = zero
    pl.semaphore_wait(barrier, 22)
    for n in range(22):
        note(n, note_slots(n)[0]).start()

    def loads(n):
        c = pair_of(n, x, y)
        abuf, bbuf = (a0, b0) if n % 2 == 0 else (a1, b1)
        pieces = (
            (ga.at[c], abuf),
            (gb.at[2 * c], bbuf.at[pl.ds(0, TILE)]),
            (gb.at[2 * c + 1], bbuf.at[pl.ds(TILE, TILE)]),
        )
        return [
            pltpu.make_async_copy(piece, to, load_sem.at[n % 2, t])
            for t, (piece, to) in enumerate(pieces)
        ]

    def whole(ref, index):
        return jnp.concatenate([ref[index * PER + t] for t in range(PER)], axis=0)

    def work(n, i):
        c = pair_of(n, x, y)
        abuf, bbuf = (a0, b0) if n % 2 == 0 else (a1, b1)
        sums = [None] * KEPT
        for e in range(SLOTS):
            k = words[c, 0, i * SLOTS + e]
            pos = words[c, 0, 16 + i * SLOTS + e]
            local = jnp.maximum(k - c * SPAN, 0)
            half = local // ROWS
            spot = (local - half * ROWS) * SLOTS
            line = 8 + 2 * c + half
            first, second = words[line, 0, spot], words[line, 0, spot + 1]
            at_first = words[line, 0, 16 + spot] + half * PACKED
            at_second = words[line, 0, 17 + spot] + half * PACKED
            left = whole(abuf, pos)
            for p in range(KEPT):
                j = jnp.where(k >= 0, kept[i, p], -2)
                index = jnp.where(first == j, at_first, jnp.where(second == j, at_second, 2 * PACKED))
                right = whole(bbuf, index)
                term = jnp.dot(left, right, preferred_element_type=jnp.float32)
                sums[p] = term if sums[p] is None else sums[p] + term
        for p in range(KEPT):
            if n == 0:
                acc[i * KEPT + p] = sums[p]
            else:
                acc[i * KEPT + p] += sums[p]

    def result(i):
        piece = pl.ds(i * KEPT, GROUP * KEPT)
        return pltpu.make_async_copy(acc.at[piece], part.at[piece], out_sem.at[i // GROUP])

    seen = set()

    def await_all(keys):
        for key in keys:
            if key not in seen:
                incoming(key).wait_recv()
                seen.add(key)

    final = PAIRS - LEFT - 1
    for kind, what in EVENTS:
        if kind == "send":
            await_all(ITEMS[what]["pre"])
            outgoing(what).start()
        elif kind == "rows":
            for n in range(22):
                note(n, note_slots(n)[1]).wait_recv()
            words_copy = pltpu.make_async_copy(meta, words, load_sem.at[2, 0])
            words_copy.start()
            await_all([key for key in ORDER if key[0] == "A"])
            words_copy.wait()
        elif kind == "load":
            await_all(NEEDS[what])
            for copy in loads(what):
                copy.start()
        else:
            n, i = what
            if i == 0:
                for copy in loads(n):
                    copy.wait()
            lax.fori_loop(i, i + GROUP, lambda t, carry, n=n: work(n, t), None)
            if n == final:
                result(i).start()
    await_all(ORDER)
    for i in range(0, ROWS, GROUP):
        result(i).wait()
    for key in ORDER:
        outgoing(key).wait_send()
    for n in range(22):
        note(n, note_slots(n)[0]).wait_send()


def pair_of(n, x, y):
    line = turn(y, LINE_ORDER[n // 2])
    half = x // 2 if n % 2 == 0 else 1 - x // 2
    return line * 2 + half


def product_kernel(
    meta, kept, cols, flags, share, part_ref, x_ref, ga, gb,
    out_ref, trace_ref,
    abuf, bbuf, acc, sem,
):
    i = pl.program_id(0)
    x, y, z, core = place()

    def loads(n):
        c = pair_of(PAIRS - LEFT + n, x, y)
        return [
            pltpu.make_async_copy(ga.at[c], abuf.at[n], sem.at[n, 0]),
            pltpu.make_async_copy(gb.at[2 * c], bbuf.at[n, pl.ds(0, TILE)], sem.at[n, 1]),
            pltpu.make_async_copy(gb.at[2 * c + 1], bbuf.at[n, pl.ds(TILE, TILE)], sem.at[n, 2]),
        ]

    @pl.when(i == 0)
    def _():
        for n in range(LEFT):
            for copy in loads(n):
                copy.start()
        lane = lax.broadcasted_iota(jnp.int32, (128, 1, LANES), 2)
        trace_ref[0, 0] = jnp.sum(jnp.where(lane == 0, share[...], 0.0))
        for n in range(LEFT):
            for copy in loads(n):
                copy.wait()

    acc[...] = part_ref[0]
    for n in range(LEFT):
        c = pair_of(PAIRS - LEFT + n, x, y)
        for e in range(SLOTS):
            k = meta[c, 0, i * SLOTS + e]

            @pl.when(k >= 0)
            def _(n=n, c=c, e=e, k=k):
                pos = meta[c, 0, 16 + i * SLOTS + e]
                other = k // ROWS
                for s in range(SLOTS):
                    spot = lax.rem(k, ROWS) * SLOTS + s
                    j = meta[8 + other, 0, spot]
                    p = jnp.int32(-1)
                    for t in range(KEPT):
                        p = jnp.where(kept[i, t] == j, t, p)

                    @pl.when(p >= 0)
                    def _(spot=spot, p=p):
                        at = meta[8 + other, 0, 16 + spot] + (other - 2 * c) * PACKED
                        acc[p] += jnp.dot(
                            abuf[n, pl.ds(pos * PER, PER)].reshape(BLK, BLK),
                            bbuf[n, pl.ds(at * PER, PER)].reshape(BLK, BLK),
                            preferred_element_type=jnp.float32,
                        )

    flag = flags[i] == 1
    sign = jnp.where(flag, -1.0, 1.0).astype(jnp.float32)
    for p in range(KEPT):
        j = kept[i, p]
        second = cols[i, 1] == j
        there = second | (cols[i, 0] == j)
        scale = jnp.where(flag & there, 2.0, 0.0).astype(jnp.float32)
        own = x_ref[0, second.astype(jnp.int32)].astype(jnp.float32)
        out_ref[0, p] = (scale * own + sign * acc[p]).astype(jnp.bfloat16)


def per_device(x_blocks, x_cols, out_cols, branch_flag):
    anywhere = pl.BlockSpec(memory_space=pl.ANY)
    scalars = pl.BlockSpec(memory_space=pltpu.SMEM)
    shapes = (
        jax.ShapeDtypeStruct((8, TILE, PART, BLK), jnp.bfloat16),
        jax.ShapeDtypeStruct((16, TILE, PART, BLK), jnp.bfloat16),
        jax.ShapeDtypeStruct((24, 1, LANES), jnp.int32),
        jax.ShapeDtypeStruct((128, 1, LANES), jnp.float32),
    )
    gathered = pl.pallas_call(
        pack_kernel,
        name="pack",
        out_shape=shapes,
        in_specs=[scalars, scalars, anywhere],
        out_specs=[anywhere] * 4,
        scratch_shapes=[
            pltpu.VMEM((TILE, PART, BLK), jnp.bfloat16),
            pltpu.SMEM((16,), jnp.int32),
            pltpu.VMEM((1, LANES), jnp.int32),
            pltpu.VMEM((1, LANES), jnp.float32),
            pltpu.VMEM((8, BLK), jnp.float32),
            pltpu.SemaphoreType.DMA((PACKED,)),
            pltpu.SemaphoreType.DMA((5,)),
        ],
    )(x_cols, branch_flag, x_blocks.reshape(ROWS, SLOTS, PER, PART, BLK))
    ga, gb, meta, share, part = pl.pallas_call(
        gather_kernel,
        name="gather",
        out_shape=shapes + (jax.ShapeDtypeStruct((ROWS * KEPT, BLK, BLK), jnp.float32),),
        in_specs=[scalars] + [anywhere] * 4,
        out_specs=[anywhere] * 5,
        scratch_shapes=[
            pltpu.VMEM((TILE, PART, BLK), jnp.bfloat16),
            pltpu.VMEM((TILE, PART, BLK), jnp.bfloat16),
            pltpu.VMEM((2 * TILE + PER, PART, BLK), jnp.bfloat16),
            pltpu.VMEM((2 * TILE + PER, PART, BLK), jnp.bfloat16),
            pltpu.VMEM((ROWS * KEPT, BLK, BLK), jnp.float32),
            pltpu.SMEM((24, 1, LANES), jnp.int32),
            pltpu.SemaphoreType.DMA((len(ORDER),)),
            pltpu.SemaphoreType.DMA((len(ORDER),)),
            pltpu.SemaphoreType.DMA((22,)),
            pltpu.SemaphoreType.DMA((22,)),
            pltpu.SemaphoreType.DMA((3, 3)),
            pltpu.SemaphoreType.DMA((ROWS // GROUP,)),
        ],
        input_output_aliases={1: 0, 2: 1, 3: 2, 4: 3},
        compiler_params=pltpu.CompilerParams(collective_id=0, has_side_effects=True),
    )(out_cols, *gathered)
    purified, trace = pl.pallas_call(
        product_kernel,
        name="product",
        grid=(ROWS,),
        out_shape=(
            jax.ShapeDtypeStruct((ROWS, KEPT, BLK, BLK), jnp.bfloat16),
            jax.ShapeDtypeStruct((1, 1), jnp.float32),
        ),
        in_specs=[
            scalars, scalars, scalars, scalars,
            pl.BlockSpec((128, 1, LANES), lambda i: (0, 0, 0)),
            pl.BlockSpec((1, KEPT, BLK, BLK), lambda i: (i, 0, 0, 0)),
            pl.BlockSpec((1, SLOTS, BLK, BLK), lambda i: (i, 0, 0, 0)),
            anywhere, anywhere,
        ],
        out_specs=[pl.BlockSpec((1, KEPT, BLK, BLK), lambda i: (i, 0, 0, 0)), scalars],
        scratch_shapes=[
            pltpu.VMEM((LEFT, TILE, PART, BLK), jnp.bfloat16),
            pltpu.VMEM((LEFT, 2 * TILE, PART, BLK), jnp.bfloat16),
            pltpu.VMEM((KEPT, BLK, BLK), jnp.float32),
            pltpu.SemaphoreType.DMA((LEFT, 3)),
        ],
    )(meta, out_cols, x_cols, branch_flag, share,
      part.reshape(ROWS, KEPT, BLK, BLK), x_blocks, ga, gb)
    return purified, trace.reshape(1)


def solution(mesh):
    in_specs = (P("row", "col", None, None), P("row", "col"), P("row", "col"), P("row"))
    out_specs = (P("row", "col", None, None), P())
    return jax.shard_map(
        per_device, mesh=mesh, in_specs=in_specs, out_specs=out_specs, check_vma=False
    )
```

```python
import jax
import jax.numpy as jnp
from jax import lax
from jax.experimental import pallas as pl
from jax.experimental.pallas import tpu as pltpu
from jax.sharding import PartitionSpec as P

MESH = pl.DeviceIdType.MESH
BLK = 256
ROWS = 8
SLOTS = 2
KEPT = 4
PACKED = 13
PART = 64
PER = BLK // PART
TILE = PACKED * PER
CUT = TILE // 4
RING = 4
SPAN = 16
LANES = 128
LOOKAHEAD = 0.4


def build_plan():
    items = {}
    step = {"x+": (1, 0), "x-": (-1, 0), "y+": (0, 1), "y-": (0, -1)}

    for q in range(4):
        first, second = ("x", "y") if q < 2 else ("y", "x")
        arrived = {(0, 0): None}

        def send(link, off):
            key = ("B", link, off[0] % RING, off[1] % RING, q)
            pre = arrived[(off[0] % RING, off[1] % RING)]
            items[key] = dict(link=link, size=1.0, pre=[pre] if pre else [])
            move = step[link]
            arrived[((off[0] - move[0]) % RING, (off[1] - move[1]) % RING)] = key

        def line(axis, base):
            unit = (1, 0) if axis == "x" else (0, 1)
            send(axis + "+", base)
            send(axis + "-", base)
            if q % 2 == 0:
                send(axis + "+", (base[0] - unit[0], base[1] - unit[1]))
            else:
                send(axis + "-", (base[0] + unit[0], base[1] + unit[1]))

        line(first, (0, 0))
        for off in range(RING):
            line(second, (off, 0) if first == "x" else (0, off))

    for q in range(4):
        items[("A", "z+", 0, q)] = dict(link="z+", size=1.0, pre=[])
        items[("A", "z-", 0, q)] = dict(link="z-", size=1.0, pre=[])
        if q % 2 == 0:
            items[("A", "z+", 3, q)] = dict(link="z+", size=1.0, pre=[("A", "z+", 0, q)])
            far = ("A", "z+", 3, q)
        else:
            items[("A", "z-", 1, q)] = dict(link="z-", size=1.0, pre=[("A", "z-", 0, q)])
            far = ("A", "z-", 1, q)
        items[("A", "s", 0, q)] = dict(link="s", size=0.2, pre=[])
        items[("A", "s", 3, q)] = dict(link="s", size=0.2, pre=[("A", "z+", 0, q)])
        items[("A", "s", 1, q)] = dict(link="s", size=0.2, pre=[("A", "z-", 0, q)])
        items[("A", "s", 2, q)] = dict(link="s", size=0.2, pre=[far])

    before = []
    for axis in "xyz":
        items[("M", axis + "+", 0)] = dict(link=axis + "+", size=0.02, pre=list(before))
        items[("M", axis + "-", 0)] = dict(link=axis + "-", size=0.02, pre=list(before))
        items[("M", axis + "+", 3)] = dict(link=axis + "+", size=0.02, pre=[("M", axis + "+", 0)])
        before = before + [("M", axis + "+", 0), ("M", axis + "-", 0), ("M", axis + "+", 3)]
    items[("M", "s", 0)] = dict(link="s", size=0.02, pre=list(before))

    source = {}
    for key in items:
        if key[0] == "B":
            move = step[key[1]]
            source[((key[2] - move[0]) % RING, (key[3] - move[1]) % RING, key[4])] = key

    def group(dx, dy):
        return 2 * LINE_ORDER.index(dy) + (1 if dx == 2 else 0)

    due = {key: float(PAIRS * 2) for key in items}
    for (dx, dy, q), key in source.items():
        due[key] = DEADLINES[group(dx, dy)]
    after = {key: [] for key in items}
    for key, item in items.items():
        for pre in item["pre"]:
            after[pre].append(key)
    rank = {}

    def urgency(key):
        if key not in rank:
            rank[key] = min(
                [due[key]] + [urgency(k) - items[k]["size"] - SLACK for k in after[key]]
            )
        return rank[key]

    free = {item["link"]: 0.0 for item in items.values()}
    start, landed = {}, {}
    todo = list(items)
    while todo:
        best = None
        for key in todo:
            if any(pre not in landed for pre in items[key]["pre"]):
                continue
            ready = max([landed[pre] + SLACK for pre in items[key]["pre"]] or [0.0])
            if key[0] == "M":
                ready = max(ready, SHARE_AT)
            at = max(ready, free[items[key]["link"]])
            small = 0 if key[0] == "M" else 1
            mark = (at, small, urgency(key))
            if best is None or mark < best[0]:
                best = (mark, key, ready, at)
        _, key, ready, at = best
        todo.remove(key)
        start[key] = (max(ready, at - LOOKAHEAD), at, len(start))
        free[items[key]["link"]] = at + items[key]["size"]
        landed[key] = at + items[key]["size"]
    events = [(start[key], ("send", key)) for key in items]

    events.append(((0.4, 0.0, 0), ("trace", None)))
    events.append(((SHARE_AT - LOOKAHEAD - 0.1, 0.0, 0), ("share", None)))

    clock = max(landed[key] for key in items if key[0] == "A") + 0.2
    events.append(((clock, 0.0, 0), ("rows", None)))
    needs = []
    for n in range(PAIRS - LEFT):
        need = [key for (dx, dy, q), key in source.items() if group(dx, dy) <= n
                and group(dx, dy) // 2 == n // 2]
        needs.append(need)
        there = max([landed[key] for key in need]) + 0.2
        began = max(clock - (0.4 if n else 0.0), there)
        events.append(((began, 0.5, n), ("load", n)))
        clock = max(clock, began + 0.3)
        for i in range(0, ROWS, GROUP):
            events.append(((clock, 1.0, i), ("work", (n, i))))
            clock = clock + CHUNK * GROUP
    events.sort()
    order = sorted(items, key=lambda key: start[key])
    return [event for _, event in events], order, items, needs, max(landed.values()), clock


PAIRS = 8
SHARE_AT = 3.0
LEFT = 1
LINE_ORDER = (0, 1, 3, 2)
DEADLINES = (2.0, 3.0, 6.0, 7.0, 10.0, 11.0, 14.0, 15.0)
SLACK = 0.5
CHUNK = 0.13
GROUP = 4
EVENTS, ORDER, ITEMS, NEEDS, PLAN_SLOTS, PLAN_WORK = build_plan()
NUMBER = {key: index for index, key in enumerate(ORDER)}


def place():
    row = lax.axis_index("row")
    col = lax.axis_index("col")
    return lax.rem(row, RING), row // RING, col // 2, lax.rem(col, 2)


def turn(value, by):
    return lax.rem(value + by % RING, RING)


def pack_kernel(cols, x_ref, ga, gb, meta, buf, source, line, in_sem, out_sem):
    row = lax.axis_index("row")
    col = lax.axis_index("col")
    for t in range(PACKED):
        source[t] = 0
    lane = lax.broadcasted_iota(jnp.int32, (1, LANES), 1)
    count = jnp.int32(0)
    info = jnp.zeros((1, LANES), jnp.int32)
    for s in range(ROWS * SLOTS):
        entry = cols[s % SLOTS, s // SLOTS]
        live = entry >= 0

        @pl.when(live)
        def _(s=s, count=count):
            source[count] = s

        info = jnp.where(lane == s, entry, info)
        info = jnp.where(lane == 16 + s, jnp.where(live, count, 0), info)
        count = count + live.astype(jnp.int32)

    def fetch(t):
        return pltpu.make_async_copy(
            x_ref.at[pl.ds(source[t] * PER, PER)], buf.at[pl.ds(t * PER, PER)], in_sem.at[t]
        )

    for t in range(PACKED):
        fetch(t).start()
    line[...] = info
    outs = []
    for t in range(PACKED):
        fetch(t).wait()
        piece = pl.ds(t * PER, PER)
        for n, to in enumerate((gb.at[row, piece], ga.at[col, piece])):
            copy = pltpu.make_async_copy(buf.at[piece], to, out_sem.at[2 * t + n])
            copy.start()
            outs.append(copy)
    for n, slot in enumerate((col, 8 + row)):
        copy = pltpu.make_async_copy(line, meta.at[slot], out_sem.at[2 * PACKED + n])
        copy.start()
        outs.append(copy)
    for copy in outs:
        copy.wait()


def gather_kernel(
    kept, cols, flags, x_ref, ga_in, gb_in, meta_in, ga, gb, meta, share, part,
    a0, a1, b0, b1, own, acc, words, total, norm, send_sem, recv_sem, note_send, note_recv, load_sem, out_sem,
):
    row = lax.axis_index("row")
    col = lax.axis_index("col")
    x, y, z, core = place()

    def peer(link):
        by = 1 if link.endswith("+") else -1
        if link[0] == "x":
            return {"row": y * RING + turn(x, by), "col": z * 2 + core}
        if link[0] == "y":
            return {"row": turn(y, by) * RING + x, "col": z * 2 + core}
        if link[0] == "z":
            return {"row": y * RING + x, "col": turn(z, by) * 2 + core}
        return {"row": y * RING + x, "col": z * 2 + 1 - core}

    def region(key, at):
        px, py, pz, pcore = at
        if key[0] == "B":
            slot = turn(py, key[3]) * RING + turn(px, key[2])
            return gb.at[slot, pl.ds(key[4] * CUT, CUT)]
        if key[0] == "A":
            slot = turn(pz, key[2]) * 2 + pcore
            return ga.at[slot, pl.ds(key[3] * CUT, CUT)]
        axis = key[1][0]
        if axis == "x":
            return share.at[pl.ds(pcore * 64 + pz * 16 + py * 4 + turn(px, key[2]), 1)]
        if axis == "y":
            return share.at[pl.ds(pcore * 64 + pz * 16 + turn(py, key[2]) * 4, 4)]
        if axis == "z":
            return share.at[pl.ds(pcore * 64 + turn(pz, key[2]) * 16, 16)]
        return share.at[pl.ds(pcore * 64, 64)]

    def outgoing(key):
        piece = region(key, (x, y, z, core))
        n = NUMBER[key]
        return pltpu.make_async_remote_copy(
            src_ref=piece,
            dst_ref=piece,
            send_sem=send_sem.at[n],
            recv_sem=recv_sem.at[n],
            device_id=peer(key[1]),
            device_id_type=MESH,
        )

    def incoming(key):
        link = key[1]
        by = -1 if link.endswith("+") else 1
        at = (x, y, z, core)
        if link[0] == "x":
            at = (turn(x, by), y, z, core)
        elif link[0] == "y":
            at = (x, turn(y, by), z, core)
        elif link[0] == "z":
            at = (x, y, turn(z, by), core)
        else:
            at = (x, y, z, 1 - core)
        piece = region(key, at)
        n = NUMBER[key]
        return pltpu.make_async_remote_copy(
            src_ref=piece,
            dst_ref=piece,
            send_sem=send_sem.at[n],
            recv_sem=recv_sem.at[n],
            device_id=peer(link),
            device_id_type=MESH,
        )

    def note_slots(n):
        if n < 7:
            return col, lax.rem(col + 7 - n, 8)
        return 8 + row, 8 + lax.rem(row + 22 - n, 16)

    def note_device(n):
        if n < 7:
            return {"row": row, "col": lax.rem(col + n + 1, 8)}
        return {"row": lax.rem(row + n - 6, 16), "col": col}

    def note(n, slot):
        return pltpu.make_async_remote_copy(
            src_ref=meta.at[slot],
            dst_ref=meta.at[slot],
            send_sem=note_send.at[n],
            recv_sem=note_recv.at[n],
            device_id=note_device(n),
            device_id_type=MESH,
        )

    barrier = pltpu.get_barrier_semaphore()
    for n in range(22):
        pl.semaphore_signal(barrier, inc=1, device_id=note_device(n), device_id_type=MESH)
    zero = jnp.zeros((PART, BLK), jnp.bfloat16)
    for t in range(PER):
        b0[2 * TILE + t] = zero
        b1[2 * TILE + t] = zero
    own_copy = pltpu.make_async_copy(x_ref, own, load_sem.at[2, 1])
    own_copy.start()
    pl.semaphore_wait(barrier, 22)
    for n in range(22):
        note(n, note_slots(n)[0]).start()

    def loads(n):
        c = pair_of(n, x, y)
        abuf, bbuf = (a0, b0) if n % 2 == 0 else (a1, b1)
        pieces = (
            (ga.at[c], abuf),
            (gb.at[2 * c], bbuf.at[pl.ds(0, TILE)]),
            (gb.at[2 * c + 1], bbuf.at[pl.ds(TILE, TILE)]),
        )
        return [
            pltpu.make_async_copy(piece, to, load_sem.at[n % 2, t])
            for t, (piece, to) in enumerate(pieces)
        ]

    def whole(ref, index):
        return jnp.concatenate([ref[index * PER + t] for t in range(PER)], axis=0)

    def work(n, i):
        c = pair_of(n, x, y)
        abuf, bbuf = (a0, b0) if n % 2 == 0 else (a1, b1)
        sums = [None] * KEPT
        for e in range(SLOTS):
            k = words[c, 0, i * SLOTS + e]
            pos = words[c, 0, 16 + i * SLOTS + e]
            local = jnp.maximum(k - c * SPAN, 0)
            half = local // ROWS
            spot = (local - half * ROWS) * SLOTS
            line = 8 + 2 * c + half
            first, second = words[line, 0, spot], words[line, 0, spot + 1]
            at_first = words[line, 0, 16 + spot] + half * PACKED
            at_second = words[line, 0, 17 + spot] + half * PACKED
            left = whole(abuf, pos)
            for p in range(KEPT):
                j = jnp.where(k >= 0, kept[p, i], -2)
                index = jnp.where(first == j, at_first, jnp.where(second == j, at_second, 2 * PACKED))
                right = whole(bbuf, index)
                term = jnp.dot(left, right, preferred_element_type=jnp.float32)
                sums[p] = term if sums[p] is None else sums[p] + term
        flag = flags[i] == 1
        sign = jnp.where(flag, -1.0, 1.0).astype(jnp.float32)
        for p in range(KEPT):
            if n == 0:
                second = cols[1, i] == kept[p, i]
                there = second | (cols[0, i] == kept[p, i])
                scale = jnp.where(flag & there, 2.0, 0.0).astype(jnp.float32)
                block = whole(own, i * SLOTS + jnp.where(second, 1, 0)).astype(jnp.float32)
                acc[i * KEPT + p] = scale * block + sign * sums[p]
            else:
                acc[i * KEPT + p] += sign * sums[p]

    def norms(i, carry):
        sign = jnp.where(flags[i] == 1, -1.0, 1.0).astype(jnp.float32)
        for s in range(SLOTS):
            entry = cols[s, i]
            weight = jnp.where(entry >= 0, sign, 0.0)
            twice = jnp.where((flags[i] == 1) & (entry == row * ROWS + i), 2.0, 0.0)
            block = whole(own, i * SLOTS + s).astype(jnp.float32)
            down = lax.broadcasted_iota(jnp.int32, (BLK, BLK), 0)
            across = lax.broadcasted_iota(jnp.int32, (BLK, BLK), 1)
            term = weight * block * block + jnp.where(down == across, twice * block, 0.0)
            norm[...] += jnp.sum(term.reshape(BLK // 8, 8, BLK), axis=0)
        return carry

    share_copy = pltpu.make_async_copy(
        total, share.at[core * 64 + z * 16 + y * 4 + x], load_sem.at[2, 2]
    )

    def result(i):
        piece = pl.ds(i * KEPT, GROUP * KEPT)
        return pltpu.make_async_copy(acc.at[piece], part.at[piece], out_sem.at[i // GROUP])

    seen = set()

    def await_all(keys):
        for key in keys:
            if key not in seen:
                incoming(key).wait_recv()
                seen.add(key)

    final = PAIRS - LEFT - 1
    for kind, what in EVENTS:
        if kind == "send":
            await_all(ITEMS[what]["pre"])
            outgoing(what).start()
        elif kind == "trace":
            own_copy.wait()
            norm[...] = jnp.zeros_like(norm)
            lax.fori_loop(0, ROWS, norms, 0)
            lane = lax.broadcasted_iota(jnp.int32, (1, LANES), 1)
            total[...] = jnp.where(lane == 0, jnp.sum(norm[...]), 0.0)
        elif kind == "share":
            share_copy.start()
            share_copy.wait()
        elif kind == "rows":
            for n in range(22):
                note(n, note_slots(n)[1]).wait_recv()
            words_copy = pltpu.make_async_copy(meta, words, load_sem.at[2, 0])
            words_copy.start()
            await_all([key for key in ORDER if key[0] == "A"])
            words_copy.wait()
        elif kind == "load":
            await_all(NEEDS[what])
            for copy in loads(what):
                copy.start()
        else:
            n, i = what
            if i == 0:
                for copy in loads(n):
                    copy.wait()
            lax.fori_loop(i, i + GROUP, lambda t, carry, n=n: work(n, t), None)
            if n == final:
                result(i).start()
    await_all(ORDER)
    for i in range(0, ROWS, GROUP):
        result(i).wait()
    for key in ORDER:
        outgoing(key).wait_send()
    for n in range(22):
        note(n, note_slots(n)[0]).wait_send()


def pair_of(n, x, y):
    line = turn(y, LINE_ORDER[n // 2])
    half = x // 2 if n % 2 == 0 else 1 - x // 2
    return line * 2 + half


def product_kernel(
    meta, kept, flags, share, part_ref, ga, gb, out_ref, trace_ref, abuf, bbuf, sem
):
    i = pl.program_id(0)
    x, y, z, core = place()
    c = pair_of(PAIRS - 1, x, y)

    def loads():
        return [
            pltpu.make_async_copy(ga.at[c], abuf, sem.at[0]),
            pltpu.make_async_copy(gb.at[2 * c], bbuf.at[pl.ds(0, TILE)], sem.at[1]),
            pltpu.make_async_copy(gb.at[2 * c + 1], bbuf.at[pl.ds(TILE, TILE)], sem.at[2]),
        ]

    @pl.when(i == 0)
    def _():
        for copy in loads():
            copy.start()
        bbuf[pl.ds(2 * TILE, PER)] = jnp.zeros((PER, PART, BLK), jnp.bfloat16)
        lane = lax.broadcasted_iota(jnp.int32, (128, 1, LANES), 2)
        trace_ref[0, 0] = jnp.sum(jnp.where(lane == 0, share[...], 0.0))
        for copy in loads():
            copy.wait()

    sign = jnp.where(flags[i] == 1, -1.0, 1.0).astype(jnp.float32)
    lines = []
    for e in range(SLOTS):
        k = meta[c, 0, i * SLOTS + e]
        pos = meta[c, 0, 16 + i * SLOTS + e]
        local = jnp.maximum(k - c * SPAN, 0)
        half = local // ROWS
        spot = (local - half * ROWS) * SLOTS
        line = 8 + 2 * c + half
        at = [meta[line, 0, 16 + spot + t] + half * PACKED for t in range(SLOTS)]
        lines.append((k >= 0, pos, [meta[line, 0, spot + t] for t in range(SLOTS)], at))
    for p in range(KEPT):
        j = kept[p, i]
        spots, hits = [], []
        for live, _, names, at in lines:
            first, second = live & (names[0] == j), live & (names[1] == j)
            spots.append(jnp.where(first, at[0], jnp.where(second, at[1], 2 * PACKED)))
            hits.append(first | second)

        @pl.when(hits[0] | hits[1])
        def _(p=p, spots=spots):
            terms = [
                jnp.dot(
                    abuf[pl.ds(line[1] * PER, PER)].reshape(BLK, BLK),
                    bbuf[pl.ds(spot * PER, PER)].reshape(BLK, BLK),
                    preferred_element_type=jnp.float32,
                )
                for line, spot in zip(lines, spots)
            ]
            out_ref[0, p] = (part_ref[0, p] + sign * (terms[0] + terms[1])).astype(jnp.bfloat16)

        @pl.when(jnp.logical_not(hits[0] | hits[1]))
        def _(p=p):
            out_ref[0, p] = part_ref[0, p].astype(jnp.bfloat16)


def per_device(x_blocks, x_cols, out_cols, branch_flag):
    anywhere = pl.BlockSpec(memory_space=pl.ANY)
    scalars = pl.BlockSpec(memory_space=pltpu.SMEM)
    cols, kept = x_cols.T, out_cols.T
    blocks = x_blocks.reshape(ROWS * SLOTS * PER, PART, BLK)
    shapes = (
        jax.ShapeDtypeStruct((8, TILE, PART, BLK), jnp.bfloat16),
        jax.ShapeDtypeStruct((16, TILE, PART, BLK), jnp.bfloat16),
        jax.ShapeDtypeStruct((24, 1, LANES), jnp.int32),
    )
    gathered = pl.pallas_call(
        pack_kernel,
        name="pack",
        out_shape=shapes,
        in_specs=[scalars, anywhere],
        out_specs=[anywhere] * 3,
        scratch_shapes=[
            pltpu.VMEM((TILE, PART, BLK), jnp.bfloat16),
            pltpu.SMEM((16,), jnp.int32),
            pltpu.VMEM((1, LANES), jnp.int32),
            pltpu.SemaphoreType.DMA((PACKED,)),
            pltpu.SemaphoreType.DMA((2 * PACKED + 2,)),
        ],
    )(cols, blocks)
    ga, gb, meta, share, part = pl.pallas_call(
        gather_kernel,
        name="gather",
        out_shape=shapes + (
            jax.ShapeDtypeStruct((128, 1, LANES), jnp.float32),
            jax.ShapeDtypeStruct((ROWS * KEPT, BLK, BLK), jnp.float32),
        ),
        in_specs=[scalars] * 3 + [anywhere] * 4,
        out_specs=[anywhere] * 5,
        scratch_shapes=[
            pltpu.VMEM((TILE, PART, BLK), jnp.bfloat16),
            pltpu.VMEM((TILE, PART, BLK), jnp.bfloat16),
            pltpu.VMEM((2 * TILE + PER, PART, BLK), jnp.bfloat16),
            pltpu.VMEM((2 * TILE + PER, PART, BLK), jnp.bfloat16),
            pltpu.VMEM((ROWS * SLOTS * PER, PART, BLK), jnp.bfloat16),
            pltpu.VMEM((ROWS * KEPT, BLK, BLK), jnp.float32),
            pltpu.SMEM((24, 1, LANES), jnp.int32),
            pltpu.VMEM((1, LANES), jnp.float32),
            pltpu.VMEM((8, BLK), jnp.float32),
            pltpu.SemaphoreType.DMA((len(ORDER),)),
            pltpu.SemaphoreType.DMA((len(ORDER),)),
            pltpu.SemaphoreType.DMA((22,)),
            pltpu.SemaphoreType.DMA((22,)),
            pltpu.SemaphoreType.DMA((3, 3)),
            pltpu.SemaphoreType.DMA((ROWS // GROUP,)),
        ],
        input_output_aliases={4: 0, 5: 1, 6: 2},
        compiler_params=pltpu.CompilerParams(collective_id=0, has_side_effects=True),
    )(kept, cols, branch_flag, blocks, *gathered)
    purified, trace = pl.pallas_call(
        product_kernel,
        name="product",
        grid=(ROWS,),
        out_shape=(
            jax.ShapeDtypeStruct((ROWS, KEPT, BLK, BLK), jnp.bfloat16),
            jax.ShapeDtypeStruct((1, 1), jnp.float32),
        ),
        in_specs=[
            scalars, scalars, scalars,
            pl.BlockSpec((128, 1, LANES), lambda i: (0, 0, 0)),
            pl.BlockSpec((1, KEPT, BLK, BLK), lambda i: (i, 0, 0, 0)),
            anywhere, anywhere,
        ],
        out_specs=[pl.BlockSpec((1, KEPT, BLK, BLK), lambda i: (i, 0, 0, 0)), scalars],
        scratch_shapes=[
            pltpu.VMEM((TILE, PART, BLK), jnp.bfloat16),
            pltpu.VMEM((2 * TILE + PER, PART, BLK), jnp.bfloat16),
            pltpu.SemaphoreType.DMA((3,)),
        ],
    )(meta, kept, branch_flag, share, part.reshape(ROWS, KEPT, BLK, BLK), ga, gb)
    return purified, trace.reshape(1)


def solution(mesh):
    in_specs = (P("row", "col", None, None), P("row", "col"), P("row", "col"), P("row"))
    out_specs = (P("row", "col", None, None), P())
    return jax.shard_map(
        per_device, mesh=mesh, in_specs=in_specs, out_specs=out_specs, check_vma=False
    )
```

```python
import jax
import jax.numpy as jnp
from jax import lax
from jax.experimental import pallas as pl
from jax.experimental.pallas import tpu as pltpu
from jax.sharding import PartitionSpec as P

MESH = pl.DeviceIdType.MESH
BLK = 256
ROWS = 8
SLOTS = 2
KEPT = 4
PACKED = 13
PART = 64
PER = BLK // PART
TILE = PACKED * PER
CUT = TILE // 4
RING = 4
SPAN = 16
LANES = 128
LOOKAHEAD = 0.4


def build_plan():
    items = {}
    step = {"x+": (1, 0), "x-": (-1, 0), "y+": (0, 1), "y-": (0, -1)}

    for q in range(4):
        first, second = ("x", "y") if q < 2 else ("y", "x")
        arrived = {(0, 0): None}

        def send(link, off):
            key = ("B", link, off[0] % RING, off[1] % RING, q)
            pre = arrived[(off[0] % RING, off[1] % RING)]
            items[key] = dict(link=link, size=1.0, pre=[pre] if pre else [])
            move = step[link]
            arrived[((off[0] - move[0]) % RING, (off[1] - move[1]) % RING)] = key

        def line(axis, base):
            unit = (1, 0) if axis == "x" else (0, 1)
            send(axis + "+", base)
            send(axis + "-", base)
            if q % 2 == 0:
                send(axis + "+", (base[0] - unit[0], base[1] - unit[1]))
            else:
                send(axis + "-", (base[0] + unit[0], base[1] + unit[1]))

        line(first, (0, 0))
        for off in range(RING):
            line(second, (off, 0) if first == "x" else (0, off))

    for q in range(4):
        items[("A", "z+", 0, q)] = dict(link="z+", size=1.0, pre=[])
        items[("A", "z-", 0, q)] = dict(link="z-", size=1.0, pre=[])
        if q % 2 == 0:
            items[("A", "z+", 3, q)] = dict(link="z+", size=1.0, pre=[("A", "z+", 0, q)])
            far = ("A", "z+", 3, q)
        else:
            items[("A", "z-", 1, q)] = dict(link="z-", size=1.0, pre=[("A", "z-", 0, q)])
            far = ("A", "z-", 1, q)
        items[("A", "s", 0, q)] = dict(link="s", size=0.2, pre=[])
        items[("A", "s", 3, q)] = dict(link="s", size=0.2, pre=[("A", "z+", 0, q)])
        items[("A", "s", 1, q)] = dict(link="s", size=0.2, pre=[("A", "z-", 0, q)])
        items[("A", "s", 2, q)] = dict(link="s", size=0.2, pre=[far])

    before = []
    for axis in "xyz":
        items[("M", axis + "+", 0)] = dict(link=axis + "+", size=0.02, pre=list(before))
        items[("M", axis + "-", 0)] = dict(link=axis + "-", size=0.02, pre=list(before))
        items[("M", axis + "+", 3)] = dict(link=axis + "+", size=0.02, pre=[("M", axis + "+", 0)])
        before = before + [("M", axis + "+", 0), ("M", axis + "-", 0), ("M", axis + "+", 3)]
    items[("M", "s", 0)] = dict(link="s", size=0.02, pre=list(before))

    for axis in "xyz":
        pre = [("N", "x+", 0), ("N", "x-", 0), ("N", "x+", 3)] if axis == "y" else []
        items[("N", axis + "+", 0)] = dict(link=axis + "+", size=0.02, pre=pre)
        items[("N", axis + "-", 0)] = dict(link=axis + "-", size=0.02, pre=pre)
        items[("N", axis + "+", 3)] = dict(link=axis + "+", size=0.02, pre=[("N", axis + "+", 0)])
    items[("N", "s", 0)] = dict(
        link="s", size=0.02, pre=[("N", "z+", 0), ("N", "z-", 0), ("N", "z+", 3)]
    )

    source = {}
    for key in items:
        if key[0] == "B":
            move = step[key[1]]
            source[((key[2] - move[0]) % RING, (key[3] - move[1]) % RING, key[4])] = key

    def group(dx, dy):
        return 2 * LINE_ORDER.index(dy) + (1 if dx == 2 else 0)

    due = {key: float(PAIRS * 2) for key in items}
    for (dx, dy, q), key in source.items():
        due[key] = DEADLINES[group(dx, dy)]
    after = {key: [] for key in items}
    for key, item in items.items():
        for pre in item["pre"]:
            after[pre].append(key)
    rank = {}

    def urgency(key):
        if key not in rank:
            rank[key] = min(
                [due[key]] + [urgency(k) - items[k]["size"] - SLACK for k in after[key]]
            )
        return rank[key]

    free = {item["link"]: 0.0 for item in items.values()}
    start, landed = {}, {}
    todo = list(items)
    while todo:
        best = None
        for key in todo:
            if any(pre not in landed for pre in items[key]["pre"]):
                continue
            ready = max([landed[pre] + SLACK for pre in items[key]["pre"]] or [0.0])
            if key[0] == "M":
                ready = max(ready, SHARE_AT)
            at = max(ready, free[items[key]["link"]])
            small = 0 if key[0] in "MN" else 1
            mark = (at, small, urgency(key))
            if best is None or mark < best[0]:
                best = (mark, key, ready, at)
        _, key, ready, at = best
        todo.remove(key)
        start[key] = (max(ready, at - LOOKAHEAD), at, len(start))
        free[items[key]["link"]] = at + items[key]["size"]
        landed[key] = at + items[key]["size"]
    events = [(start[key], ("send", key)) for key in items]

    events.append(((0.4, 0.0, 0), ("trace", None)))
    events.append(((SHARE_AT - LOOKAHEAD - 0.1, 0.0, 0), ("share", None)))

    clock = max(landed[key] for key in items if key[0] in "AN") + 0.2
    events.append(((clock, 0.0, 0), ("rows", None)))
    needs = []
    for n in range(PAIRS - LEFT):
        need = [key for (dx, dy, q), key in source.items() if group(dx, dy) <= n
                and group(dx, dy) // 2 == n // 2]
        needs.append(need)
        there = max([landed[key] for key in need]) + 0.2
        began = max(clock - (0.4 if n else 0.0), there)
        events.append(((began, 0.5, n), ("load", n)))
        clock = max(clock, began + 0.3)
        for i in range(0, ROWS, GROUP):
            events.append(((clock, 1.0, i), ("work", (n, i))))
            clock = clock + CHUNK * GROUP
    events.sort()
    order = sorted(items, key=lambda key: start[key])
    return [event for _, event in events], order, items, needs, max(landed.values()), clock


PAIRS = 8
SHARE_AT = 3.0
LEFT = 1
LINE_ORDER = (0, 1, 3, 2)
DEADLINES = (2.0, 3.0, 6.0, 7.0, 10.0, 11.0, 14.0, 15.0)
SLACK = 0.5
CHUNK = 0.13
GROUP = 4
EVENTS, ORDER, ITEMS, NEEDS, PLAN_SLOTS, PLAN_WORK = build_plan()
NUMBER = {key: index for index, key in enumerate(ORDER)}


def place():
    row = lax.axis_index("row")
    col = lax.axis_index("col")
    return lax.rem(row, RING), row // RING, col // 2, lax.rem(col, 2)


def note_slot(col):
    return lax.rem(col, 2) * RING + col // 2


def turn(value, by):
    return lax.rem(value + by % RING, RING)


def pack_kernel(cols, x_ref, ga, gb, meta, buf, source, line, in_sem, out_sem):
    row = lax.axis_index("row")
    col = lax.axis_index("col")
    for t in range(PACKED):
        source[t] = 0
    lane = lax.broadcasted_iota(jnp.int32, (1, LANES), 1)
    count = jnp.int32(0)
    info = jnp.zeros((1, LANES), jnp.int32)
    for s in range(ROWS * SLOTS):
        entry = cols[s % SLOTS, s // SLOTS]
        live = entry >= 0

        @pl.when(live)
        def _(s=s, count=count):
            source[count] = s

        info = jnp.where(lane == s, entry, info)
        info = jnp.where(lane == 16 + s, jnp.where(live, count, 0), info)
        count = count + live.astype(jnp.int32)

    def fetch(t):
        return pltpu.make_async_copy(
            x_ref.at[pl.ds(source[t] * PER, PER)], buf.at[pl.ds(t * PER, PER)], in_sem.at[t]
        )

    for t in range(PACKED):
        fetch(t).start()
    line[...] = info
    outs = []
    for t in range(PACKED):
        fetch(t).wait()
        piece = pl.ds(t * PER, PER)
        for n, to in enumerate((gb.at[row, piece], ga.at[col, piece])):
            copy = pltpu.make_async_copy(buf.at[piece], to, out_sem.at[2 * t + n])
            copy.start()
            outs.append(copy)
    for n, slot in enumerate((note_slot(col), 8 + row)):
        copy = pltpu.make_async_copy(line, meta.at[slot], out_sem.at[2 * PACKED + n])
        copy.start()
        outs.append(copy)
    for copy in outs:
        copy.wait()


def gather_kernel(
    kept, cols, flags, x_ref, ga_in, gb_in, meta_in, ga, gb, meta, share, part, draft,
    a0, a1, b0, b1, own, acc, rounded, words, total, norm, send_sem, recv_sem, load_sem, out_sem,
):
    row = lax.axis_index("row")
    col = lax.axis_index("col")
    x, y, z, core = place()

    def peer(link):
        by = 1 if link.endswith("+") else -1
        if link[0] == "x":
            return {"row": y * RING + turn(x, by), "col": z * 2 + core}
        if link[0] == "y":
            return {"row": turn(y, by) * RING + x, "col": z * 2 + core}
        if link[0] == "z":
            return {"row": y * RING + x, "col": turn(z, by) * 2 + core}
        return {"row": y * RING + x, "col": z * 2 + 1 - core}

    def region(key, at):
        px, py, pz, pcore = at
        if key[0] == "B":
            slot = turn(py, key[3]) * RING + turn(px, key[2])
            return gb.at[slot, pl.ds(key[4] * CUT, CUT)]
        if key[0] == "A":
            slot = turn(pz, key[2]) * 2 + pcore
            return ga.at[slot, pl.ds(key[3] * CUT, CUT)]
        axis = key[1][0]
        if key[0] == "N":
            if axis == "x":
                return meta.at[pl.ds(8 + py * 4 + turn(px, key[2]), 1)]
            if axis == "y":
                return meta.at[pl.ds(8 + turn(py, key[2]) * 4, 4)]
            if axis == "z":
                return meta.at[pl.ds(pcore * 4 + turn(pz, key[2]), 1)]
            return meta.at[pl.ds(pcore * 4, 4)]
        if axis == "x":
            return share.at[pl.ds(pcore * 64 + pz * 16 + py * 4 + turn(px, key[2]), 1)]
        if axis == "y":
            return share.at[pl.ds(pcore * 64 + pz * 16 + turn(py, key[2]) * 4, 4)]
        if axis == "z":
            return share.at[pl.ds(pcore * 64 + turn(pz, key[2]) * 16, 16)]
        return share.at[pl.ds(pcore * 64, 64)]

    def outgoing(key):
        piece = region(key, (x, y, z, core))
        n = NUMBER[key]
        return pltpu.make_async_remote_copy(
            src_ref=piece,
            dst_ref=piece,
            send_sem=send_sem.at[n],
            recv_sem=recv_sem.at[n],
            device_id=peer(key[1]),
            device_id_type=MESH,
        )

    def incoming(key):
        link = key[1]
        by = -1 if link.endswith("+") else 1
        at = (x, y, z, core)
        if link[0] == "x":
            at = (turn(x, by), y, z, core)
        elif link[0] == "y":
            at = (x, turn(y, by), z, core)
        elif link[0] == "z":
            at = (x, y, turn(z, by), core)
        else:
            at = (x, y, z, 1 - core)
        piece = region(key, at)
        n = NUMBER[key]
        return pltpu.make_async_remote_copy(
            src_ref=piece,
            dst_ref=piece,
            send_sem=send_sem.at[n],
            recv_sem=recv_sem.at[n],
            device_id=peer(link),
            device_id_type=MESH,
        )

    barrier = pltpu.get_barrier_semaphore()
    links = ("x+", "x-", "y+", "y-", "z+", "z-", "s")
    for link in links:
        pl.semaphore_signal(barrier, inc=1, device_id=peer(link), device_id_type=MESH)
    zero = jnp.zeros((PART, BLK), jnp.bfloat16)
    for t in range(PER):
        b0[2 * TILE + t] = zero
        b1[2 * TILE + t] = zero
    own_copy = pltpu.make_async_copy(x_ref, own, load_sem.at[2, 1])
    own_copy.start()
    pl.semaphore_wait(barrier, len(links))

    def loads(n):
        c = pair_of(n, x, y)
        abuf, bbuf = (a0, b0) if n % 2 == 0 else (a1, b1)
        pieces = (
            (ga.at[c], abuf),
            (gb.at[2 * c], bbuf.at[pl.ds(0, TILE)]),
            (gb.at[2 * c + 1], bbuf.at[pl.ds(TILE, TILE)]),
        )
        return [
            pltpu.make_async_copy(piece, to, load_sem.at[n % 2, t])
            for t, (piece, to) in enumerate(pieces)
        ]

    def whole(ref, index):
        return jnp.concatenate([ref[index * PER + t] for t in range(PER)], axis=0)

    def work(n, i):
        c = pair_of(n, x, y)
        abuf, bbuf = (a0, b0) if n % 2 == 0 else (a1, b1)
        sums = [None] * KEPT
        for e in range(SLOTS):
            k = words[note_slot(c), 0, i * SLOTS + e]
            pos = words[note_slot(c), 0, 16 + i * SLOTS + e]
            local = jnp.maximum(k - c * SPAN, 0)
            half = local // ROWS
            spot = (local - half * ROWS) * SLOTS
            line = 8 + 2 * c + half
            first, second = words[line, 0, spot], words[line, 0, spot + 1]
            at_first = words[line, 0, 16 + spot] + half * PACKED
            at_second = words[line, 0, 17 + spot] + half * PACKED
            left = whole(abuf, pos)
            for p in range(KEPT):
                j = jnp.where(k >= 0, kept[p, i], -2)
                index = jnp.where(first == j, at_first, jnp.where(second == j, at_second, 2 * PACKED))
                right = whole(bbuf, index)
                term = jnp.dot(left, right, preferred_element_type=jnp.float32)
                sums[p] = term if sums[p] is None else sums[p] + term
        flag = flags[i] == 1
        sign = jnp.where(flag, -1.0, 1.0).astype(jnp.float32)
        for p in range(KEPT):
            if n == 0:
                second = cols[1, i] == kept[p, i]
                there = second | (cols[0, i] == kept[p, i])
                scale = jnp.where(flag & there, 2.0, 0.0).astype(jnp.float32)
                block = whole(own, i * SLOTS + jnp.where(second, 1, 0)).astype(jnp.float32)
                acc[i * KEPT + p] = scale * block + sign * sums[p]
            else:
                acc[i * KEPT + p] += sign * sums[p]
            if n == PAIRS - LEFT - 1:
                rounded[i * KEPT + p] = acc[i * KEPT + p].astype(jnp.bfloat16)

    def norms(i, carry):
        sign = jnp.where(flags[i] == 1, -1.0, 1.0).astype(jnp.float32)
        for s in range(SLOTS):
            entry = cols[s, i]
            weight = jnp.where(entry >= 0, sign, 0.0)
            twice = jnp.where((flags[i] == 1) & (entry == row * ROWS + i), 2.0, 0.0)
            block = whole(own, i * SLOTS + s).astype(jnp.float32)
            down = lax.broadcasted_iota(jnp.int32, (BLK, BLK), 0)
            across = lax.broadcasted_iota(jnp.int32, (BLK, BLK), 1)
            term = weight * block * block + jnp.where(down == across, twice * block, 0.0)
            norm[...] += jnp.sum(term.reshape(BLK // 8, 8, BLK), axis=0)
        return carry

    share_copy = pltpu.make_async_copy(
        total, share.at[core * 64 + z * 16 + y * 4 + x], load_sem.at[2, 2]
    )

    def result(i):
        piece = pl.ds(i * KEPT, GROUP * KEPT)
        return [
            pltpu.make_async_copy(acc.at[piece], part.at[piece], out_sem.at[i // GROUP, 0]),
            pltpu.make_async_copy(rounded.at[piece], draft.at[piece], out_sem.at[i // GROUP, 1]),
        ]

    seen = set()

    def await_all(keys):
        for key in keys:
            if key not in seen:
                incoming(key).wait_recv()
                seen.add(key)

    final = PAIRS - LEFT - 1
    for kind, what in EVENTS:
        if kind == "send":
            await_all(ITEMS[what]["pre"])
            outgoing(what).start()
        elif kind == "trace":
            own_copy.wait()
            norm[...] = jnp.zeros_like(norm)
            lax.fori_loop(0, ROWS, norms, 0)
            lane = lax.broadcasted_iota(jnp.int32, (1, LANES), 1)
            total[...] = jnp.where(lane == 0, jnp.sum(norm[...]), 0.0)
        elif kind == "share":
            share_copy.start()
            share_copy.wait()
        elif kind == "rows":
            await_all([key for key in ORDER if key[0] == "N"])
            words_copy = pltpu.make_async_copy(meta, words, load_sem.at[2, 0])
            words_copy.start()
            await_all([key for key in ORDER if key[0] == "A"])
            words_copy.wait()
        elif kind == "load":
            await_all(NEEDS[what])
            for copy in loads(what):
                copy.start()
        else:
            n, i = what
            if i == 0:
                for copy in loads(n):
                    copy.wait()
            lax.fori_loop(i, i + GROUP, lambda t, carry, n=n: work(n, t), None)
            if n == final:
                for copy in result(i):
                    copy.start()
    await_all(ORDER)
    for i in range(0, ROWS, GROUP):
        for copy in result(i):
            copy.wait()
    for key in ORDER:
        outgoing(key).wait_send()


def pair_of(n, x, y):
    line = turn(y, LINE_ORDER[n // 2])
    half = x // 2 if n % 2 == 0 else 1 - x // 2
    return line * 2 + half


def product_kernel(
    meta, kept, flags, share, draft_ref, part, ga, gb, out_ref, trace_ref, abuf, bbuf, sums, sem
):
    i = pl.program_id(0)
    x, y, z, core = place()
    c = pair_of(PAIRS - 1, x, y)

    def each(local, visit_left, visit_sum, visit_right):
        lines = []
        for e in range(SLOTS):
            k = meta[note_slot(c), 0, local * SLOTS + e]
            inside = jnp.maximum(k - c * SPAN, 0)
            half = inside // ROWS
            spot = (inside - half * ROWS) * SLOTS
            line = 8 + 2 * c + half
            names = [jnp.where(k >= 0, meta[line, 0, spot + t], -1) for t in range(SLOTS)]
            at = [meta[line, 0, 16 + spot + t] for t in range(SLOTS)]
            lines.append((2 * c + half, names, at))
        hits = []
        for p in range(KEPT):
            j = kept[p, local]
            hits.append([(names[0] == j, names[1] == j) for _, names, _ in lines])
        for e in range(SLOTS):
            some = hits[0][e][0] | hits[0][e][1]
            for p in range(1, KEPT):
                some = some | hits[p][e][0] | hits[p][e][1]

            @pl.when(some)
            def _(e=e):
                visit_left(e, meta[note_slot(c), 0, 16 + local * SLOTS + e])

        for p in range(KEPT):
            found = [first | second for first, second in hits[p]]

            @pl.when(found[0] | found[1])
            def _(p=p, found=found):
                visit_sum(p)
                for e in range(SLOTS):

                    @pl.when(found[e])
                    def _(e=e):
                        tile, _, at = lines[e]
                        visit_right(p, e, tile, jnp.where(hits[p][e][0], at[0], at[1]))

    def left(local, e, pos):
        return pltpu.make_async_copy(
            ga.at[c, pl.ds(pos * PER, PER)], abuf.at[local * SLOTS + e], sem.at[local]
        )

    def before(local, p):
        n = local * KEPT + p
        return pltpu.make_async_copy(part.at[n], sums.at[n], sem.at[local])

    def right(local, p, e, tile, pos):
        return pltpu.make_async_copy(
            gb.at[tile, pl.ds(pos * PER, PER)],
            bbuf.at[(local * KEPT + p) * SLOTS + e],
            sem.at[local],
        )

    def over(local, act):
        each(
            local,
            lambda e, pos: act(left(local, e, pos)),
            lambda p: act(before(local, p)),
            lambda p, e, tile, pos: act(right(local, p, e, tile, pos)),
        )

    @pl.when(i == 0)
    def _():
        def begin(local, carry):
            over(local, lambda copy: copy.start())
            return carry

        lax.fori_loop(0, ROWS, begin, 0)
        lane = lax.broadcasted_iota(jnp.int32, (128, 1, LANES), 2)
        trace_ref[0, 0] = jnp.sum(jnp.where(lane == 0, share[...], 0.0))

    over(i, lambda copy: copy.wait())
    out_ref[...] = draft_ref[...]
    sign = jnp.where(flags[i] == 1, -1.0, 1.0).astype(jnp.float32)

    def multiply(p, e, tile, pos):
        n = i * KEPT + p
        total = sums[n] + sign * jnp.dot(
            abuf[i * SLOTS + e].reshape(BLK, BLK),
            bbuf[n * SLOTS + e].reshape(BLK, BLK),
            preferred_element_type=jnp.float32,
        )
        sums[n] = total
        out_ref[0, p] = total.astype(jnp.bfloat16)

    each(i, lambda e, pos: None, lambda p: None, multiply)


def per_device(x_blocks, x_cols, out_cols, branch_flag):
    anywhere = pl.BlockSpec(memory_space=pl.ANY)
    scalars = pl.BlockSpec(memory_space=pltpu.SMEM)
    cols, kept = x_cols.T, out_cols.T
    blocks = x_blocks.reshape(ROWS * SLOTS * PER, PART, BLK)
    shapes = (
        jax.ShapeDtypeStruct((8, TILE, PART, BLK), jnp.bfloat16),
        jax.ShapeDtypeStruct((16, TILE, PART, BLK), jnp.bfloat16),
        jax.ShapeDtypeStruct((24, 1, LANES), jnp.int32),
    )
    gathered = pl.pallas_call(
        pack_kernel,
        name="pack",
        out_shape=shapes,
        in_specs=[scalars, anywhere],
        out_specs=[anywhere] * 3,
        scratch_shapes=[
            pltpu.VMEM((TILE, PART, BLK), jnp.bfloat16),
            pltpu.SMEM((16,), jnp.int32),
            pltpu.VMEM((1, LANES), jnp.int32),
            pltpu.SemaphoreType.DMA((PACKED,)),
            pltpu.SemaphoreType.DMA((2 * PACKED + 2,)),
        ],
    )(cols, blocks)
    ga, gb, meta, share, part, draft = pl.pallas_call(
        gather_kernel,
        name="gather",
        out_shape=shapes + (
            jax.ShapeDtypeStruct((128, 1, LANES), jnp.float32),
            jax.ShapeDtypeStruct((ROWS * KEPT, BLK, BLK), jnp.float32),
            jax.ShapeDtypeStruct((ROWS * KEPT, BLK, BLK), jnp.bfloat16),
        ),
        in_specs=[scalars] * 3 + [anywhere] * 4,
        out_specs=[anywhere] * 6,
        scratch_shapes=[
            pltpu.VMEM((TILE, PART, BLK), jnp.bfloat16),
            pltpu.VMEM((TILE, PART, BLK), jnp.bfloat16),
            pltpu.VMEM((2 * TILE + PER, PART, BLK), jnp.bfloat16),
            pltpu.VMEM((2 * TILE + PER, PART, BLK), jnp.bfloat16),
            pltpu.VMEM((ROWS * SLOTS * PER, PART, BLK), jnp.bfloat16),
            pltpu.VMEM((ROWS * KEPT, BLK, BLK), jnp.float32),
            pltpu.VMEM((ROWS * KEPT, BLK, BLK), jnp.bfloat16),
            pltpu.SMEM((24, 1, LANES), jnp.int32),
            pltpu.VMEM((1, LANES), jnp.float32),
            pltpu.VMEM((8, BLK), jnp.float32),
            pltpu.SemaphoreType.DMA((len(ORDER),)),
            pltpu.SemaphoreType.DMA((len(ORDER),)),
            pltpu.SemaphoreType.DMA((3, 3)),
            pltpu.SemaphoreType.DMA((ROWS // GROUP, 2)),
        ],
        input_output_aliases={4: 0, 5: 1, 6: 2},
        compiler_params=pltpu.CompilerParams(collective_id=0, has_side_effects=True),
    )(kept, cols, branch_flag, blocks, *gathered)
    purified, trace = pl.pallas_call(
        product_kernel,
        name="product",
        grid=(ROWS,),
        out_shape=(
            jax.ShapeDtypeStruct((ROWS, KEPT, BLK, BLK), jnp.bfloat16),
            jax.ShapeDtypeStruct((1, 1), jnp.float32),
        ),
        in_specs=[
            scalars, scalars, scalars,
            pl.BlockSpec((128, 1, LANES), lambda i: (0, 0, 0)),
            pl.BlockSpec((1, KEPT, BLK, BLK), lambda i: (i, 0, 0, 0)),
            anywhere, anywhere, anywhere,
        ],
        out_specs=[pl.BlockSpec((1, KEPT, BLK, BLK), lambda i: (i, 0, 0, 0)), scalars],
        scratch_shapes=[
            pltpu.VMEM((ROWS * SLOTS, PER, PART, BLK), jnp.bfloat16),
            pltpu.VMEM((ROWS * KEPT * SLOTS, PER, PART, BLK), jnp.bfloat16),
            pltpu.VMEM((ROWS * KEPT, BLK, BLK), jnp.float32),
            pltpu.SemaphoreType.DMA((ROWS,)),
        ],
    )(meta, kept, branch_flag, share, draft.reshape(ROWS, KEPT, BLK, BLK), part, ga, gb)
    return purified, trace.reshape(1)


def solution(mesh):
    in_specs = (P("row", "col", None, None), P("row", "col"), P("row", "col"), P("row"))
    out_specs = (P("row", "col", None, None), P())
    return jax.shard_map(
        per_device, mesh=mesh, in_specs=in_specs, out_specs=out_specs, check_vma=False
    )
```

```python
import jax
import jax.numpy as jnp
from jax import lax
from jax.experimental import pallas as pl
from jax.experimental.pallas import tpu as pltpu
from jax.sharding import PartitionSpec as P

MESH = pl.DeviceIdType.MESH
BLK = 256
ROWS = 8
SLOTS = 2
KEPT = 4
PACKED = 13
PART = 64
PER = BLK // PART
TILE = PACKED * PER
CUT = TILE // 4
RING = 4
SPAN = 16
LANES = 128
LOOKAHEAD = 0.4


def build_plan():
    items = {}
    step = {"x+": (1, 0), "x-": (-1, 0), "y+": (0, 1), "y-": (0, -1)}

    for q in range(4):
        first, second = ("x", "y") if q < 2 else ("y", "x")
        arrived = {(0, 0): None}

        def send(link, off):
            key = ("B", link, off[0] % RING, off[1] % RING, q)
            pre = arrived[(off[0] % RING, off[1] % RING)]
            items[key] = dict(link=link, size=1.0, pre=[pre] if pre else [])
            move = step[link]
            arrived[((off[0] - move[0]) % RING, (off[1] - move[1]) % RING)] = key

        def line(axis, base):
            unit = (1, 0) if axis == "x" else (0, 1)
            send(axis + "+", base)
            send(axis + "-", base)
            if q % 2 == 0:
                send(axis + "+", (base[0] - unit[0], base[1] - unit[1]))
            else:
                send(axis + "-", (base[0] + unit[0], base[1] + unit[1]))

        line(first, (0, 0))
        for off in range(RING):
            line(second, (off, 0) if first == "x" else (0, off))

    for q in range(4):
        items[("A", "z+", 0, q)] = dict(link="z+", size=1.0, pre=[])
        items[("A", "z-", 0, q)] = dict(link="z-", size=1.0, pre=[])
        if q % 2 == 0:
            items[("A", "z+", 3, q)] = dict(link="z+", size=1.0, pre=[("A", "z+", 0, q)])
            far = ("A", "z+", 3, q)
        else:
            items[("A", "z-", 1, q)] = dict(link="z-", size=1.0, pre=[("A", "z-", 0, q)])
            far = ("A", "z-", 1, q)
        items[("A", "s", 0, q)] = dict(link="s", size=0.2, pre=[])
        items[("A", "s", 3, q)] = dict(link="s", size=0.2, pre=[("A", "z+", 0, q)])
        items[("A", "s", 1, q)] = dict(link="s", size=0.2, pre=[("A", "z-", 0, q)])
        items[("A", "s", 2, q)] = dict(link="s", size=0.2, pre=[far])

    before = []
    for axis in "xyz":
        items[("M", axis + "+", 0)] = dict(link=axis + "+", size=0.02, pre=list(before))
        items[("M", axis + "-", 0)] = dict(link=axis + "-", size=0.02, pre=list(before))
        items[("M", axis + "+", 3)] = dict(link=axis + "+", size=0.02, pre=[("M", axis + "+", 0)])
        before = before + [("M", axis + "+", 0), ("M", axis + "-", 0), ("M", axis + "+", 3)]
    items[("M", "s", 0)] = dict(link="s", size=0.02, pre=list(before))

    for axis in "xyz":
        pre = [("N", "x+", 0), ("N", "x-", 0), ("N", "x+", 3)] if axis == "y" else []
        items[("N", axis + "+", 0)] = dict(link=axis + "+", size=0.02, pre=pre)
        items[("N", axis + "-", 0)] = dict(link=axis + "-", size=0.02, pre=pre)
        items[("N", axis + "+", 3)] = dict(link=axis + "+", size=0.02, pre=[("N", axis + "+", 0)])
    items[("N", "s", 0)] = dict(
        link="s", size=0.02, pre=[("N", "z+", 0), ("N", "z-", 0), ("N", "z+", 3)]
    )

    source = {}
    for key in items:
        if key[0] == "B":
            move = step[key[1]]
            source[((key[2] - move[0]) % RING, (key[3] - move[1]) % RING, key[4])] = key

    def group(dx, dy):
        return 2 * LINE_ORDER.index(dy) + (1 if dx == 2 else 0)

    due = {key: float(PAIRS * 2) for key in items}
    for (dx, dy, q), key in source.items():
        due[key] = DEADLINES[group(dx, dy)]
    after = {key: [] for key in items}
    for key, item in items.items():
        for pre in item["pre"]:
            after[pre].append(key)
    rank = {}

    def urgency(key):
        if key not in rank:
            rank[key] = min(
                [due[key]] + [urgency(k) - items[k]["size"] - SLACK for k in after[key]]
            )
        return rank[key]

    free = {item["link"]: 0.0 for item in items.values()}
    start, landed = {}, {}
    todo = list(items)
    while todo:
        best = None
        for key in todo:
            if any(pre not in landed for pre in items[key]["pre"]):
                continue
            ready = max([landed[pre] + SLACK for pre in items[key]["pre"]] or [0.0])
            if key[0] == "M":
                ready = max(ready, SHARE_AT)
            at = max(ready, free[items[key]["link"]])
            small = 0 if key[0] in "MN" else 1
            mark = (at, small, urgency(key))
            if best is None or mark < best[0]:
                best = (mark, key, ready, at)
        _, key, ready, at = best
        todo.remove(key)
        start[key] = (max(ready, at - LOOKAHEAD), at, len(start))
        free[items[key]["link"]] = at + items[key]["size"]
        landed[key] = at + items[key]["size"]
    events = [(start[key], ("send", key)) for key in items]

    events.append(((0.4, 0.0, 0), ("trace", None)))
    events.append(((SHARE_AT - LOOKAHEAD - 0.1, 0.0, 0), ("share", None)))

    clock = max(landed[key] for key in items if key[0] in "AN") + 0.2
    events.append(((clock, 0.0, 0), ("rows", None)))
    needs = []
    for n in range(PAIRS - LEFT):
        need = [key for (dx, dy, q), key in source.items() if group(dx, dy) <= n
                and group(dx, dy) // 2 == n // 2]
        needs.append(need)
        there = max([landed[key] for key in need]) + 0.2
        began = max(clock - (0.4 if n else 0.0), there)
        events.append(((began, 0.5, n), ("load", n)))
        clock = max(clock, began + 0.3)
        for i in range(0, ROWS, GROUP):
            events.append(((clock, 1.0, i), ("work", (n, i))))
            clock = clock + CHUNK * GROUP
    events.sort()
    order = sorted(items, key=lambda key: start[key])
    return [event for _, event in events], order, items, needs, max(landed.values()), clock


PAIRS = 8
SHARE_AT = 3.0
LEFT = 1
LINE_ORDER = (0, 1, 3, 2)
DEADLINES = (2.0, 3.0, 6.0, 7.0, 10.0, 11.0, 14.0, 15.0)
SLACK = 0.5
CHUNK = 0.13
GROUP = 4
EVENTS, ORDER, ITEMS, NEEDS, PLAN_SLOTS, PLAN_WORK = build_plan()
NUMBER = {key: index for index, key in enumerate(ORDER)}


def place():
    row = lax.axis_index("row")
    col = lax.axis_index("col")
    return lax.rem(row, RING), row // RING, col // 2, lax.rem(col, 2)


def note_slot(col):
    return lax.rem(col, 2) * RING + col // 2


def turn(value, by):
    return lax.rem(value + by % RING, RING)


def gather_kernel(
    kept, cols, flags, x_ref, ga, gb, meta, share, part, draft,
    a0, a1, b0, b1, own, packed, line, acc, rounded, words, total, norm, send_sem, recv_sem, load_sem, out_sem,
):
    row = lax.axis_index("row")
    col = lax.axis_index("col")
    x, y, z, core = place()

    def peer(link):
        by = 1 if link.endswith("+") else -1
        if link[0] == "x":
            return {"row": y * RING + turn(x, by), "col": z * 2 + core}
        if link[0] == "y":
            return {"row": turn(y, by) * RING + x, "col": z * 2 + core}
        if link[0] == "z":
            return {"row": y * RING + x, "col": turn(z, by) * 2 + core}
        return {"row": y * RING + x, "col": z * 2 + 1 - core}

    def region(key, at):
        px, py, pz, pcore = at
        if key[0] == "B":
            slot = turn(py, key[3]) * RING + turn(px, key[2])
            return gb.at[slot, pl.ds(key[4] * CUT, CUT)]
        if key[0] == "A":
            slot = turn(pz, key[2]) * 2 + pcore
            return ga.at[slot, pl.ds(key[3] * CUT, CUT)]
        axis = key[1][0]
        if key[0] == "N":
            if axis == "x":
                return meta.at[pl.ds(8 + py * 4 + turn(px, key[2]), 1)]
            if axis == "y":
                return meta.at[pl.ds(8 + turn(py, key[2]) * 4, 4)]
            if axis == "z":
                return meta.at[pl.ds(pcore * 4 + turn(pz, key[2]), 1)]
            return meta.at[pl.ds(pcore * 4, 4)]
        if axis == "x":
            return share.at[pl.ds(pcore * 64 + pz * 16 + py * 4 + turn(px, key[2]), 1)]
        if axis == "y":
            return share.at[pl.ds(pcore * 64 + pz * 16 + turn(py, key[2]) * 4, 4)]
        if axis == "z":
            return share.at[pl.ds(pcore * 64 + turn(pz, key[2]) * 16, 16)]
        return share.at[pl.ds(pcore * 64, 64)]

    def outgoing(key):
        piece = region(key, (x, y, z, core))
        n = NUMBER[key]
        return pltpu.make_async_remote_copy(
            src_ref=piece,
            dst_ref=piece,
            send_sem=send_sem.at[n],
            recv_sem=recv_sem.at[n],
            device_id=peer(key[1]),
            device_id_type=MESH,
        )

    def incoming(key):
        link = key[1]
        by = -1 if link.endswith("+") else 1
        at = (x, y, z, core)
        if link[0] == "x":
            at = (turn(x, by), y, z, core)
        elif link[0] == "y":
            at = (x, turn(y, by), z, core)
        elif link[0] == "z":
            at = (x, y, turn(z, by), core)
        else:
            at = (x, y, z, 1 - core)
        piece = region(key, at)
        n = NUMBER[key]
        return pltpu.make_async_remote_copy(
            src_ref=piece,
            dst_ref=piece,
            send_sem=send_sem.at[n],
            recv_sem=recv_sem.at[n],
            device_id=peer(link),
            device_id_type=MESH,
        )

    barrier = pltpu.get_barrier_semaphore()
    links = ("x+", "x-", "y+", "y-", "z+", "z-", "s")
    for link in links:
        pl.semaphore_signal(barrier, inc=1, device_id=peer(link), device_id_type=MESH)
    own_copy = pltpu.make_async_copy(x_ref, own, load_sem.at[2, 1])
    own_copy.start()

    lane = lax.broadcasted_iota(jnp.int32, (1, LANES), 1)
    count = jnp.int32(0)
    info = jnp.zeros((1, LANES), jnp.int32)
    source = [jnp.int32(0)] * PACKED
    for s in range(ROWS * SLOTS):
        entry = cols[s % SLOTS, s // SLOTS]
        live = entry >= 0
        info = jnp.where(lane == s, entry, info)
        info = jnp.where(lane == 16 + s, jnp.where(live & (count < PACKED), count, 0), info)
        for t in range(max(0, s - ROWS * SLOTS + 1), min(s + 1, PACKED)):
            source[t] = jnp.where(live & (count == t), s, source[t])
        count = count + jnp.where(live, 1, 0)
    line[...] = info
    own_copy.wait()
    for t in range(PACKED):
        for h in range(PER):
            packed[t * PER + h] = own[source[t] * PER + h]
    zero = jnp.zeros((PART, BLK), jnp.bfloat16)
    for t in range(PER):
        b0[2 * TILE + t] = zero
        b1[2 * TILE + t] = zero
    norm[...] = jnp.zeros_like(norm)
    first = [
        pltpu.make_async_copy(line, meta.at[note_slot(col)], load_sem.at[0, 0]),
        pltpu.make_async_copy(line, meta.at[8 + row], load_sem.at[0, 1]),
        pltpu.make_async_copy(packed, gb.at[row], load_sem.at[1, 0]),
        pltpu.make_async_copy(packed, ga.at[col], load_sem.at[1, 1]),
    ]
    for copy in first:
        copy.start()
    pl.semaphore_wait(barrier, len(links))
    for copy in first:
        copy.wait()

    def loads(n):
        c = pair_of(n, x, y)
        abuf, bbuf = (a0, b0) if n % 2 == 0 else (a1, b1)
        pieces = (
            (ga.at[c], abuf),
            (gb.at[2 * c], bbuf.at[pl.ds(0, TILE)]),
            (gb.at[2 * c + 1], bbuf.at[pl.ds(TILE, TILE)]),
        )
        return [
            pltpu.make_async_copy(piece, to, load_sem.at[n % 2, t])
            for t, (piece, to) in enumerate(pieces)
        ]

    def whole(ref, index):
        return jnp.concatenate([ref[index * PER + t] for t in range(PER)], axis=0)

    def work(n, i):
        c = pair_of(n, x, y)
        abuf, bbuf = (a0, b0) if n % 2 == 0 else (a1, b1)
        sums = [None] * KEPT
        for e in range(SLOTS):
            k = words[note_slot(c), 0, i * SLOTS + e]
            pos = words[note_slot(c), 0, 16 + i * SLOTS + e]
            local = jnp.maximum(k - c * SPAN, 0)
            half = local // ROWS
            spot = (local - half * ROWS) * SLOTS
            line = 8 + 2 * c + half
            first, second = words[line, 0, spot], words[line, 0, spot + 1]
            at_first = words[line, 0, 16 + spot] + half * PACKED
            at_second = words[line, 0, 17 + spot] + half * PACKED
            left = whole(abuf, pos)
            for p in range(KEPT):
                j = jnp.where(k >= 0, kept[p, i], -2)
                index = jnp.where(first == j, at_first, jnp.where(second == j, at_second, 2 * PACKED))
                right = whole(bbuf, index)
                term = jnp.dot(left, right, preferred_element_type=jnp.float32)
                sums[p] = term if sums[p] is None else sums[p] + term
        flag = flags[i] == 1
        sign = jnp.where(flag, -1.0, 1.0).astype(jnp.float32)
        for p in range(KEPT):
            if n == 0:
                second = cols[1, i] == kept[p, i]
                there = second | (cols[0, i] == kept[p, i])
                scale = jnp.where(flag & there, 2.0, 0.0).astype(jnp.float32)
                block = whole(own, i * SLOTS + jnp.where(second, 1, 0)).astype(jnp.float32)
                acc[i * KEPT + p] = scale * block + sign * sums[p]
            else:
                acc[i * KEPT + p] += sign * sums[p]
            if n == PAIRS - LEFT - 1:
                rounded[i * KEPT + p] = acc[i * KEPT + p].astype(jnp.bfloat16)

    def norms(i, carry):
        sign = jnp.where(flags[i] == 1, -1.0, 1.0).astype(jnp.float32)
        for s in range(SLOTS):
            entry = cols[s, i]
            weight = jnp.where(entry >= 0, sign, 0.0)
            twice = jnp.where((flags[i] == 1) & (entry == row * ROWS + i), 2.0, 0.0)
            block = whole(own, i * SLOTS + s).astype(jnp.float32)
            down = lax.broadcasted_iota(jnp.int32, (BLK, BLK), 0)
            across = lax.broadcasted_iota(jnp.int32, (BLK, BLK), 1)
            term = weight * block * block + jnp.where(down == across, twice * block, 0.0)
            norm[...] += jnp.sum(term.reshape(BLK // 8, 8, BLK), axis=0)
        return carry

    share_copy = pltpu.make_async_copy(
        total, share.at[core * 64 + z * 16 + y * 4 + x], load_sem.at[2, 2]
    )

    def result(i):
        piece = pl.ds(i * KEPT, GROUP * KEPT)
        return [
            pltpu.make_async_copy(acc.at[piece], part.at[piece], out_sem.at[i // GROUP, 0]),
            pltpu.make_async_copy(rounded.at[piece], draft.at[piece], out_sem.at[i // GROUP, 1]),
        ]

    seen = set()

    def await_all(keys):
        for key in keys:
            if key not in seen:
                incoming(key).wait_recv()
                seen.add(key)

    final = PAIRS - LEFT - 1
    for kind, what in EVENTS:
        if kind == "send":
            await_all(ITEMS[what]["pre"])
            outgoing(what).start()
        elif kind == "trace":
            lax.fori_loop(0, ROWS, norms, 0)
            lane = lax.broadcasted_iota(jnp.int32, (1, LANES), 1)
            total[...] = jnp.where(lane == 0, jnp.sum(norm[...]), 0.0)
        elif kind == "share":
            share_copy.start()
            share_copy.wait()
        elif kind == "rows":
            await_all([key for key in ORDER if key[0] == "N"])
            words_copy = pltpu.make_async_copy(meta, words, load_sem.at[2, 0])
            words_copy.start()
            await_all([key for key in ORDER if key[0] == "A"])
            words_copy.wait()
        elif kind == "load":
            await_all(NEEDS[what])
            for copy in loads(what):
                copy.start()
        else:
            n, i = what
            if i == 0:
                for copy in loads(n):
                    copy.wait()
            lax.fori_loop(i, i + GROUP, lambda t, carry, n=n: work(n, t), None)
            if n == final:
                for copy in result(i):
                    copy.start()
    await_all(ORDER)
    for i in range(0, ROWS, GROUP):
        for copy in result(i):
            copy.wait()
    for key in ORDER:
        outgoing(key).wait_send()


def pair_of(n, x, y):
    line = turn(y, LINE_ORDER[n // 2])
    half = x // 2 if n % 2 == 0 else 1 - x // 2
    return line * 2 + half


def product_kernel(
    meta, kept, flags, share, draft, part, ga, gb, out, trace_ref,
    abuf, bbuf, sums, buf, touched, place_a, place_c, counts, in_sem, get_sem, out_sem,
):
    x, y, z, core = place()
    c = pair_of(PAIRS - 1, x, y)

    def through(i):
        piece = pl.ds(i * KEPT, KEPT)
        return pltpu.make_async_copy(draft.at[piece], buf.at[piece], in_sem.at[i])

    def write(n):
        return pltpu.make_async_copy(buf.at[n], out.at[n], out_sem)

    def block(tile, pos, to, i):
        return pltpu.make_async_copy(tile.at[pl.ds(pos * PER, PER)], to, get_sem.at[i, 0])

    def before(n, i):
        return pltpu.make_async_copy(part.at[n], sums.at[n], get_sem.at[i, 1])

    for i in range(ROWS):
        through(i).start()

    def begin(i, found):
        start = found
        lefts, blocks = jnp.int32(0), jnp.int32(0)
        for p in range(KEPT):
            touched[i * KEPT + p] = 0
        for e in range(SLOTS):
            k = meta[note_slot(c), 0, i * SLOTS + e]
            pos = meta[note_slot(c), 0, 16 + i * SLOTS + e]
            inside = jnp.maximum(k - c * SPAN, 0)
            half = inside // ROWS
            spot = (inside - half * ROWS) * SLOTS
            at = 8 + 2 * c + half
            base = found
            for t in range(SLOTS):
                j = jnp.where(k >= 0, meta[at, 0, spot + t], -1)
                p = jnp.int32(-1)
                for o in range(KEPT):
                    p = jnp.where(kept[o, i] == j, o, p)
                hit = p >= 0

                @pl.when(hit)
                def _(found=found, p=p, t=t, at=at, half=half, spot=spot, e=e):
                    n = i * KEPT + p
                    place_a[found] = i * SLOTS + e
                    place_c[found] = n
                    block(gb.at[2 * c + half], meta[at, 0, 16 + spot + t], bbuf.at[found], i).start()

                    @pl.when(touched[n] == 0)
                    def _():
                        before(n, i).start()
                        touched[n] = 1

                found = found + hit.astype(jnp.int32)

            @pl.when(found > base)
            def _(pos=pos, e=e):
                block(ga.at[c], pos, abuf.at[i * SLOTS + e], i).start()

            lefts = lefts + (found > base).astype(jnp.int32)
        for p in range(KEPT):
            blocks = blocks + touched[i * KEPT + p]
        counts[i, 0] = start
        counts[i, 1] = found
        counts[i, 2] = found - start + lefts
        counts[i, 3] = blocks
        return found

    lax.fori_loop(0, ROWS, begin, jnp.int32(0))

    def pass_on(i, carry):
        through(i).wait()
        for p in range(KEPT):

            @pl.when(touched[i * KEPT + p] == 0)
            def _(p=p):
                write(i * KEPT + p).start()

        return carry

    lax.fori_loop(0, ROWS, pass_on, 0)
    lane = lax.broadcasted_iota(jnp.int32, (128, 1, LANES), 2)
    trace_ref[0, 0] = jnp.sum(jnp.where(lane == 0, share[...], 0.0))

    def finish(i, carry):
        def drain_blocks(_, inner):
            block(ga.at[c], 0, abuf.at[0], i).wait()
            return inner

        def drain_sums(_, inner):
            before(0, i).wait()
            return inner

        lax.fori_loop(0, counts[i, 2], drain_blocks, 0)
        lax.fori_loop(0, counts[i, 3], drain_sums, 0)
        sign = jnp.where(flags[i] == 1, -1.0, 1.0).astype(jnp.float32)

        def multiply(t, inner):
            n = place_c[t]
            sums[n] += sign * jnp.dot(
                abuf[place_a[t]].reshape(BLK, BLK),
                bbuf[t].reshape(BLK, BLK),
                preferred_element_type=jnp.float32,
            )
            return inner

        lax.fori_loop(counts[i, 0], counts[i, 1], multiply, 0)
        for p in range(KEPT):

            @pl.when(touched[i * KEPT + p] == 1)
            def _(p=p):
                n = i * KEPT + p
                buf[n] = sums[n].astype(jnp.bfloat16)
                write(n).start()

        return carry

    lax.fori_loop(0, ROWS, finish, 0)
    pltpu.make_async_copy(buf, out, out_sem).wait()


def per_device(x_blocks, x_cols, out_cols, branch_flag):
    anywhere = pl.BlockSpec(memory_space=pl.ANY)
    scalars = pl.BlockSpec(memory_space=pltpu.SMEM)
    cols, kept = x_cols.T, out_cols.T
    blocks = x_blocks.reshape(ROWS * SLOTS * PER, PART, BLK)
    shapes = (
        jax.ShapeDtypeStruct((8, TILE, PART, BLK), jnp.bfloat16),
        jax.ShapeDtypeStruct((16, TILE, PART, BLK), jnp.bfloat16),
        jax.ShapeDtypeStruct((24, 1, LANES), jnp.int32),
    )
    ga, gb, meta, share, part, draft = pl.pallas_call(
        gather_kernel,
        name="gather",
        out_shape=shapes + (
            jax.ShapeDtypeStruct((128, 1, LANES), jnp.float32),
            jax.ShapeDtypeStruct((ROWS * KEPT, BLK, BLK), jnp.float32),
            jax.ShapeDtypeStruct((ROWS * KEPT, BLK, BLK), jnp.bfloat16),
        ),
        in_specs=[scalars] * 3 + [anywhere],
        out_specs=[anywhere] * 6,
        scratch_shapes=[
            pltpu.VMEM((TILE, PART, BLK), jnp.bfloat16),
            pltpu.VMEM((TILE, PART, BLK), jnp.bfloat16),
            pltpu.VMEM((2 * TILE + PER, PART, BLK), jnp.bfloat16),
            pltpu.VMEM((2 * TILE + PER, PART, BLK), jnp.bfloat16),
            pltpu.VMEM((ROWS * SLOTS * PER, PART, BLK), jnp.bfloat16),
            pltpu.VMEM((TILE, PART, BLK), jnp.bfloat16),
            pltpu.VMEM((1, LANES), jnp.int32),
            pltpu.VMEM((ROWS * KEPT, BLK, BLK), jnp.float32),
            pltpu.VMEM((ROWS * KEPT, BLK, BLK), jnp.bfloat16),
            pltpu.SMEM((24, 1, LANES), jnp.int32),
            pltpu.VMEM((1, LANES), jnp.float32),
            pltpu.VMEM((8, BLK), jnp.float32),
            pltpu.SemaphoreType.DMA((len(ORDER),)),
            pltpu.SemaphoreType.DMA((len(ORDER),)),
            pltpu.SemaphoreType.DMA((3, 3)),
            pltpu.SemaphoreType.DMA((ROWS // GROUP, 2)),
        ],
        compiler_params=pltpu.CompilerParams(collective_id=0, has_side_effects=True),
    )(kept, cols, branch_flag, blocks)
    purified, trace = pl.pallas_call(
        product_kernel,
        name="product",
        out_shape=(
            jax.ShapeDtypeStruct((ROWS * KEPT, BLK, BLK), jnp.bfloat16),
            jax.ShapeDtypeStruct((1, 1), jnp.float32),
        ),
        in_specs=[scalars] * 3 + [pl.BlockSpec(memory_space=pltpu.VMEM)] + [anywhere] * 4,
        out_specs=[anywhere, scalars],
        scratch_shapes=[
            pltpu.VMEM((ROWS * SLOTS, PER, PART, BLK), jnp.bfloat16),
            pltpu.VMEM((ROWS * SLOTS * SLOTS, PER, PART, BLK), jnp.bfloat16),
            pltpu.VMEM((ROWS * KEPT, BLK, BLK), jnp.float32),
            pltpu.VMEM((ROWS * KEPT, BLK, BLK), jnp.bfloat16),
            pltpu.SMEM((ROWS * KEPT,), jnp.int32),
            pltpu.SMEM((ROWS * SLOTS * SLOTS,), jnp.int32),
            pltpu.SMEM((ROWS * SLOTS * SLOTS,), jnp.int32),
            pltpu.SMEM((ROWS, 4), jnp.int32),
            pltpu.SemaphoreType.DMA((ROWS,)),
            pltpu.SemaphoreType.DMA((ROWS, 2)),
            pltpu.SemaphoreType.DMA,
        ],
    )(meta, kept, branch_flag, share, draft, part, ga, gb)
    return purified.reshape(ROWS, KEPT, BLK, BLK), trace.reshape(1)


def solution(mesh):
    in_specs = (P("row", "col", None, None), P("row", "col"), P("row", "col"), P("row"))
    out_specs = (P("row", "col", None, None), P())
    return jax.shard_map(
        per_device, mesh=mesh, in_specs=in_specs, out_specs=out_specs, check_vma=False
    )
```

```python
import jax
import jax.numpy as jnp
from jax import lax
from jax.experimental import pallas as pl
from jax.experimental.pallas import tpu as pltpu
from jax.sharding import PartitionSpec as P

MESH = pl.DeviceIdType.MESH
BLK = 256
ROWS = 8
SLOTS = 2
KEPT = 4
PACKED = 13
PART = 64
PER = BLK // PART
TILE = PACKED * PER
CUT = TILE // 4
RING = 4
SPAN = 16
LANES = 128
LOOKAHEAD = 0.4


def build_plan():
    items = {}
    step = {"x+": (1, 0), "x-": (-1, 0), "y+": (0, 1), "y-": (0, -1)}

    for q in range(4):
        first, second = ("x", "y") if q < 2 else ("y", "x")
        arrived = {(0, 0): None}

        def send(link, off):
            key = ("B", link, off[0] % RING, off[1] % RING, q)
            pre = arrived[(off[0] % RING, off[1] % RING)]
            items[key] = dict(link=link, size=1.0, pre=[pre] if pre else [])
            move = step[link]
            arrived[((off[0] - move[0]) % RING, (off[1] - move[1]) % RING)] = key

        def line(axis, base):
            unit = (1, 0) if axis == "x" else (0, 1)
            send(axis + "+", base)
            send(axis + "-", base)
            if q % 2 == 0:
                send(axis + "+", (base[0] - unit[0], base[1] - unit[1]))
            else:
                send(axis + "-", (base[0] + unit[0], base[1] + unit[1]))

        line(first, (0, 0))
        for off in range(RING):
            line(second, (off, 0) if first == "x" else (0, off))

    for q in range(4):
        items[("A", "z+", 0, q)] = dict(link="z+", size=1.0, pre=[])
        items[("A", "z-", 0, q)] = dict(link="z-", size=1.0, pre=[])
        if q % 2 == 0:
            items[("A", "z+", 3, q)] = dict(link="z+", size=1.0, pre=[("A", "z+", 0, q)])
            far = ("A", "z+", 3, q)
        else:
            items[("A", "z-", 1, q)] = dict(link="z-", size=1.0, pre=[("A", "z-", 0, q)])
            far = ("A", "z-", 1, q)
        items[("A", "s", 0, q)] = dict(link="s", size=0.2, pre=[])
        items[("A", "s", 3, q)] = dict(link="s", size=0.2, pre=[("A", "z+", 0, q)])
        items[("A", "s", 1, q)] = dict(link="s", size=0.2, pre=[("A", "z-", 0, q)])
        items[("A", "s", 2, q)] = dict(link="s", size=0.2, pre=[far])

    before = []
    for axis in "xyz":
        items[("M", axis + "+", 0)] = dict(link=axis + "+", size=0.02, pre=list(before))
        items[("M", axis + "-", 0)] = dict(link=axis + "-", size=0.02, pre=list(before))
        items[("M", axis + "+", 3)] = dict(link=axis + "+", size=0.02, pre=[("M", axis + "+", 0)])
        before = before + [("M", axis + "+", 0), ("M", axis + "-", 0), ("M", axis + "+", 3)]
    items[("M", "s", 0)] = dict(link="s", size=0.02, pre=list(before))

    for axis in "xyz":
        pre = [("N", "x+", 0), ("N", "x-", 0), ("N", "x+", 3)] if axis == "y" else []
        items[("N", axis + "+", 0)] = dict(link=axis + "+", size=0.02, pre=pre)
        items[("N", axis + "-", 0)] = dict(link=axis + "-", size=0.02, pre=pre)
        items[("N", axis + "+", 3)] = dict(link=axis + "+", size=0.02, pre=[("N", axis + "+", 0)])
    items[("N", "s", 0)] = dict(
        link="s", size=0.02, pre=[("N", "z+", 0), ("N", "z-", 0), ("N", "z+", 3)]
    )

    source = {}
    for key in items:
        if key[0] == "B":
            move = step[key[1]]
            source[((key[2] - move[0]) % RING, (key[3] - move[1]) % RING, key[4])] = key

    def group(dx, dy):
        return 2 * LINE_ORDER.index(dy) + (1 if dx == 2 else 0)

    due = {key: float(PAIRS * 2) for key in items}
    for (dx, dy, q), key in source.items():
        due[key] = DEADLINES[group(dx, dy)]
    after = {key: [] for key in items}
    for key, item in items.items():
        for pre in item["pre"]:
            after[pre].append(key)
    rank = {}

    def urgency(key):
        if key not in rank:
            rank[key] = min(
                [due[key]] + [urgency(k) - items[k]["size"] - SLACK for k in after[key]]
            )
        return rank[key]

    free = {item["link"]: 0.0 for item in items.values()}
    start, landed = {}, {}
    todo = list(items)
    while todo:
        best = None
        for key in todo:
            if any(pre not in landed for pre in items[key]["pre"]):
                continue
            ready = max([landed[pre] + SLACK for pre in items[key]["pre"]] or [0.0])
            if key[0] == "M":
                ready = max(ready, SHARE_AT)
            at = max(ready, free[items[key]["link"]])
            small = 0 if key[0] in "MN" else 1
            mark = (at, small, urgency(key))
            if best is None or mark < best[0]:
                best = (mark, key, ready, at)
        _, key, ready, at = best
        todo.remove(key)
        start[key] = (max(ready, at - LOOKAHEAD), at, len(start))
        free[items[key]["link"]] = at + items[key]["size"]
        landed[key] = at + items[key]["size"]
    events = [(start[key], ("send", key)) for key in items]

    events.append(((0.4, 0.0, 0), ("trace", None)))
    events.append(((SHARE_AT - LOOKAHEAD - 0.1, 0.0, 0), ("share", None)))

    clock = max(landed[key] for key in items if key[0] in "AN") + 0.2
    events.append(((clock, 0.0, 0), ("rows", None)))
    needs = []
    for n in range(PAIRS - LEFT):
        need = [key for (dx, dy, q), key in source.items() if group(dx, dy) <= n
                and group(dx, dy) // 2 == n // 2]
        needs.append(need)
        there = max([landed[key] for key in need]) + 0.2
        began = max(clock - (0.4 if n else 0.0), there)
        events.append(((began, 0.5, n), ("load", n)))
        clock = max(clock, began + 0.3)
        for i in range(0, ROWS, GROUP):
            events.append(((clock, 1.0, i), ("work", (n, i))))
            clock = clock + CHUNK * GROUP
    events.sort()
    order = sorted(items, key=lambda key: start[key])
    return [event for _, event in events], order, items, needs, max(landed.values()), clock


PAIRS = 8
SHARE_AT = 3.0
LEFT = 1
LINE_ORDER = (0, 1, 3, 2)
DEADLINES = (2.0, 3.0, 6.0, 7.0, 10.0, 11.0, 14.0, 15.0)
SLACK = 0.25
CHUNK = 0.13
GROUP = 4
EVENTS, ORDER, ITEMS, NEEDS, PLAN_SLOTS, PLAN_WORK = build_plan()
NUMBER = {key: index for index, key in enumerate(ORDER)}


def place():
    row = lax.axis_index("row")
    col = lax.axis_index("col")
    return lax.rem(row, RING), row // RING, col // 2, lax.rem(col, 2)


def note_slot(col):
    return lax.rem(col, 2) * RING + col // 2


def turn(value, by):
    return lax.rem(value + by % RING, RING)


def gather_kernel(
    kept, cols, flags, x_ref, ga, gb, meta, share, part, draft,
    a0, a1, b0, b1, own, packed, line, acc, rounded, words, total, norm, send_sem, recv_sem, load_sem, out_sem,
):
    row = lax.axis_index("row")
    col = lax.axis_index("col")
    x, y, z, core = place()

    def peer(link):
        by = 1 if link.endswith("+") else -1
        if link[0] == "x":
            return {"row": y * RING + turn(x, by), "col": z * 2 + core}
        if link[0] == "y":
            return {"row": turn(y, by) * RING + x, "col": z * 2 + core}
        if link[0] == "z":
            return {"row": y * RING + x, "col": turn(z, by) * 2 + core}
        return {"row": y * RING + x, "col": z * 2 + 1 - core}

    def region(key, at):
        px, py, pz, pcore = at
        if key[0] == "B":
            slot = turn(py, key[3]) * RING + turn(px, key[2])
            return gb.at[slot, pl.ds(key[4] * CUT, CUT)]
        if key[0] == "A":
            slot = turn(pz, key[2]) * 2 + pcore
            return ga.at[slot, pl.ds(key[3] * CUT, CUT)]
        axis = key[1][0]
        if key[0] == "N":
            if axis == "x":
                return meta.at[pl.ds(8 + py * 4 + turn(px, key[2]), 1)]
            if axis == "y":
                return meta.at[pl.ds(8 + turn(py, key[2]) * 4, 4)]
            if axis == "z":
                return meta.at[pl.ds(pcore * 4 + turn(pz, key[2]), 1)]
            return meta.at[pl.ds(pcore * 4, 4)]
        if axis == "x":
            return share.at[pl.ds(pcore * 64 + pz * 16 + py * 4 + turn(px, key[2]), 1)]
        if axis == "y":
            return share.at[pl.ds(pcore * 64 + pz * 16 + turn(py, key[2]) * 4, 4)]
        if axis == "z":
            return share.at[pl.ds(pcore * 64 + turn(pz, key[2]) * 16, 16)]
        return share.at[pl.ds(pcore * 64, 64)]

    def outgoing(key):
        piece = region(key, (x, y, z, core))
        n = NUMBER[key]
        return pltpu.make_async_remote_copy(
            src_ref=piece,
            dst_ref=piece,
            send_sem=send_sem.at[n],
            recv_sem=recv_sem.at[n],
            device_id=peer(key[1]),
            device_id_type=MESH,
        )

    def incoming(key):
        link = key[1]
        by = -1 if link.endswith("+") else 1
        at = (x, y, z, core)
        if link[0] == "x":
            at = (turn(x, by), y, z, core)
        elif link[0] == "y":
            at = (x, turn(y, by), z, core)
        elif link[0] == "z":
            at = (x, y, turn(z, by), core)
        else:
            at = (x, y, z, 1 - core)
        piece = region(key, at)
        n = NUMBER[key]
        return pltpu.make_async_remote_copy(
            src_ref=piece,
            dst_ref=piece,
            send_sem=send_sem.at[n],
            recv_sem=recv_sem.at[n],
            device_id=peer(link),
            device_id_type=MESH,
        )

    barrier = pltpu.get_barrier_semaphore()
    links = ("x+", "x-", "y+", "y-", "z+", "z-", "s")
    for link in links:
        pl.semaphore_signal(barrier, inc=1, device_id=peer(link), device_id_type=MESH)
    own_copy = pltpu.make_async_copy(x_ref, own, load_sem.at[2, 1])
    own_copy.start()

    lane = lax.broadcasted_iota(jnp.int32, (1, LANES), 1)
    count = jnp.int32(0)
    info = jnp.zeros((1, LANES), jnp.int32)
    source = [jnp.int32(0)] * PACKED
    for s in range(ROWS * SLOTS):
        entry = cols[s % SLOTS, s // SLOTS]
        live = entry >= 0
        info = jnp.where(lane == s, entry, info)
        info = jnp.where(lane == 16 + s, jnp.where(live & (count < PACKED), count, 0), info)
        for t in range(max(0, s - ROWS * SLOTS + 1), min(s + 1, PACKED)):
            source[t] = jnp.where(live & (count == t), s, source[t])
        count = count + jnp.where(live, 1, 0)
    line[...] = info
    own_copy.wait()
    for t in range(PACKED):
        for h in range(PER):
            packed[t * PER + h] = own[source[t] * PER + h]
    zero = jnp.zeros((PART, BLK), jnp.bfloat16)
    for t in range(PER):
        b0[2 * TILE + t] = zero
        b1[2 * TILE + t] = zero
    norm[...] = jnp.zeros_like(norm)
    placed = {
        "B": [pltpu.make_async_copy(packed, gb.at[row], load_sem.at[1, 0])],
        "N": [
            pltpu.make_async_copy(line, meta.at[note_slot(col)], load_sem.at[0, 0]),
            pltpu.make_async_copy(line, meta.at[8 + row], load_sem.at[0, 1]),
        ],
        "A": [pltpu.make_async_copy(packed, ga.at[col], load_sem.at[1, 1])],
    }
    for kind in "BN":
        for copy in placed[kind]:
            copy.start()
    pl.semaphore_wait(barrier, len(links))
    for copy in placed.pop("B"):
        copy.wait()
    for copy in placed["A"]:
        copy.start()

    def loads(n):
        c = pair_of(n, x, y)
        abuf, bbuf = (a0, b0) if n % 2 == 0 else (a1, b1)
        pieces = (
            (ga.at[c], abuf),
            (gb.at[2 * c], bbuf.at[pl.ds(0, TILE)]),
            (gb.at[2 * c + 1], bbuf.at[pl.ds(TILE, TILE)]),
        )
        return [
            pltpu.make_async_copy(piece, to, load_sem.at[n % 2, t])
            for t, (piece, to) in enumerate(pieces)
        ]

    def whole(ref, index):
        return jnp.concatenate([ref[index * PER + t] for t in range(PER)], axis=0)

    def work(n, i):
        c = pair_of(n, x, y)
        abuf, bbuf = (a0, b0) if n % 2 == 0 else (a1, b1)
        sums = [None] * KEPT
        for e in range(SLOTS):
            k = words[note_slot(c), 0, i * SLOTS + e]
            pos = words[note_slot(c), 0, 16 + i * SLOTS + e]
            local = jnp.maximum(k - c * SPAN, 0)
            half = local // ROWS
            spot = (local - half * ROWS) * SLOTS
            line = 8 + 2 * c + half
            first, second = words[line, 0, spot], words[line, 0, spot + 1]
            at_first = words[line, 0, 16 + spot] + half * PACKED
            at_second = words[line, 0, 17 + spot] + half * PACKED
            left = whole(abuf, pos)
            for p in range(KEPT):
                j = jnp.where(k >= 0, kept[p, i], -2)
                index = jnp.where(first == j, at_first, jnp.where(second == j, at_second, 2 * PACKED))
                right = whole(bbuf, index)
                term = jnp.dot(left, right, preferred_element_type=jnp.float32)
                sums[p] = term if sums[p] is None else sums[p] + term
        flag = flags[i] == 1
        sign = jnp.where(flag, -1.0, 1.0).astype(jnp.float32)
        for p in range(KEPT):
            if n == 0:
                second = cols[1, i] == kept[p, i]
                there = second | (cols[0, i] == kept[p, i])
                scale = jnp.where(flag & there, 2.0, 0.0).astype(jnp.float32)
                block = whole(own, i * SLOTS + jnp.where(second, 1, 0)).astype(jnp.float32)
                acc[i * KEPT + p] = scale * block + sign * sums[p]
            else:
                acc[i * KEPT + p] += sign * sums[p]
            if n == PAIRS - LEFT - 1:
                rounded[i * KEPT + p] = acc[i * KEPT + p].astype(jnp.bfloat16)

    def norms(i, carry):
        sign = jnp.where(flags[i] == 1, -1.0, 1.0).astype(jnp.float32)
        for s in range(SLOTS):
            entry = cols[s, i]
            weight = jnp.where(entry >= 0, sign, 0.0)
            twice = jnp.where((flags[i] == 1) & (entry == row * ROWS + i), 2.0, 0.0)
            block = whole(own, i * SLOTS + s).astype(jnp.float32)
            down = lax.broadcasted_iota(jnp.int32, (BLK, BLK), 0)
            across = lax.broadcasted_iota(jnp.int32, (BLK, BLK), 1)
            term = weight * block * block + jnp.where(down == across, twice * block, 0.0)
            norm[...] += jnp.sum(term.reshape(BLK // 8, 8, BLK), axis=0)
        return carry

    share_copy = pltpu.make_async_copy(
        total, share.at[core * 64 + z * 16 + y * 4 + x], load_sem.at[2, 2]
    )

    def result(i):
        piece = pl.ds(i * KEPT, GROUP * KEPT)
        return [
            pltpu.make_async_copy(acc.at[piece], part.at[piece], out_sem.at[i // GROUP, 0]),
            pltpu.make_async_copy(rounded.at[piece], draft.at[piece], out_sem.at[i // GROUP, 1]),
        ]

    seen = set()

    def await_all(keys):
        for key in keys:
            if key not in seen:
                incoming(key).wait_recv()
                seen.add(key)

    final = PAIRS - LEFT - 1
    for kind, what in EVENTS:
        if kind == "send":
            for copy in placed.pop(what[0], []):
                copy.wait()
            await_all(ITEMS[what]["pre"])
            outgoing(what).start()
        elif kind == "trace":
            lax.fori_loop(0, ROWS, norms, 0)
            lane = lax.broadcasted_iota(jnp.int32, (1, LANES), 1)
            total[...] = jnp.where(lane == 0, jnp.sum(norm[...]), 0.0)
        elif kind == "share":
            share_copy.start()
            share_copy.wait()
        elif kind == "rows":
            await_all([key for key in ORDER if key[0] == "N"])
            words_copy = pltpu.make_async_copy(meta, words, load_sem.at[2, 0])
            words_copy.start()
            await_all([key for key in ORDER if key[0] == "A"])
            words_copy.wait()
        elif kind == "load":
            await_all(NEEDS[what])
            for copy in loads(what):
                copy.start()
        else:
            n, i = what
            if i == 0:
                for copy in loads(n):
                    copy.wait()
            lax.fori_loop(i, i + GROUP, lambda t, carry, n=n: work(n, t), None)
            if n == final:
                for copy in result(i):
                    copy.start()
    await_all(ORDER)
    for i in range(0, ROWS, GROUP):
        for copy in result(i):
            copy.wait()
    for key in ORDER:
        outgoing(key).wait_send()


def pair_of(n, x, y):
    line = turn(y, LINE_ORDER[n // 2])
    half = x // 2 if n % 2 == 0 else 1 - x // 2
    return line * 2 + half


def product_kernel(
    meta, kept, flags, share, draft, part, ga, gb, out, trace_ref,
    abuf, bbuf, sums, buf, touched, place_a, place_c, counts, in_sem, get_sem, out_sem,
):
    x, y, z, core = place()
    c = pair_of(PAIRS - 1, x, y)

    def through(i):
        piece = pl.ds(i * KEPT, KEPT)
        return pltpu.make_async_copy(draft.at[piece], buf.at[piece], in_sem.at[i])

    def write(n):
        return pltpu.make_async_copy(buf.at[n], out.at[n], out_sem)

    def block(tile, pos, to, i):
        return pltpu.make_async_copy(tile.at[pl.ds(pos * PER, PER)], to, get_sem.at[i, 0])

    def before(n, i):
        return pltpu.make_async_copy(part.at[n], sums.at[n], get_sem.at[i, 1])

    for i in range(ROWS):
        through(i).start()

    def begin(i, found):
        start = found
        lefts, blocks = jnp.int32(0), jnp.int32(0)
        for p in range(KEPT):
            touched[i * KEPT + p] = 0
        for e in range(SLOTS):
            k = meta[note_slot(c), 0, i * SLOTS + e]
            pos = meta[note_slot(c), 0, 16 + i * SLOTS + e]
            inside = jnp.maximum(k - c * SPAN, 0)
            half = inside // ROWS
            spot = (inside - half * ROWS) * SLOTS
            at = 8 + 2 * c + half
            base = found
            for t in range(SLOTS):
                j = jnp.where(k >= 0, meta[at, 0, spot + t], -1)
                p = jnp.int32(-1)
                for o in range(KEPT):
                    p = jnp.where(kept[o, i] == j, o, p)
                hit = p >= 0

                @pl.when(hit)
                def _(found=found, p=p, t=t, at=at, half=half, spot=spot, e=e):
                    n = i * KEPT + p
                    place_a[found] = i * SLOTS + e
                    place_c[found] = n
                    block(gb.at[2 * c + half], meta[at, 0, 16 + spot + t], bbuf.at[found], i).start()

                    @pl.when(touched[n] == 0)
                    def _():
                        before(n, i).start()
                        touched[n] = 1

                found = found + hit.astype(jnp.int32)

            @pl.when(found > base)
            def _(pos=pos, e=e):
                block(ga.at[c], pos, abuf.at[i * SLOTS + e], i).start()

            lefts = lefts + (found > base).astype(jnp.int32)
        for p in range(KEPT):
            blocks = blocks + touched[i * KEPT + p]
        counts[i, 0] = start
        counts[i, 1] = found
        counts[i, 2] = found - start + lefts
        counts[i, 3] = blocks
        return found

    lax.fori_loop(0, ROWS, begin, jnp.int32(0))

    def pass_on(i, carry):
        through(i).wait()
        for p in range(KEPT):

            @pl.when(touched[i * KEPT + p] == 0)
            def _(p=p):
                write(i * KEPT + p).start()

        return carry

    lax.fori_loop(0, ROWS, pass_on, 0)
    lane = lax.broadcasted_iota(jnp.int32, (128, 1, LANES), 2)
    trace_ref[0, 0] = jnp.sum(jnp.where(lane == 0, share[...], 0.0))

    def term(t):
        n = place_c[t]
        sign = jnp.where(flags[n // KEPT] == 1, -1.0, 1.0).astype(jnp.float32)
        return n, sign * jnp.dot(
            abuf[place_a[t]].reshape(BLK, BLK),
            bbuf[t].reshape(BLK, BLK),
            preferred_element_type=jnp.float32,
        )

    def finish(g, carry):
        def drain_blocks(i):
            def drain(_, inner):
                block(ga.at[c], 0, abuf.at[0], i).wait()
                return inner

            lax.fori_loop(0, counts[i, 2], drain, 0)

        def drain_sums(i):
            def drain(_, inner):
                before(0, i).wait()
                return inner

            lax.fori_loop(0, counts[i, 3], drain, 0)

        for r in range(2):
            drain_blocks(2 * g + r)
            drain_sums(2 * g + r)
        start, stop = counts[2 * g, 0], counts[2 * g + 1, 1]
        half = (stop - start) // 2

        def two(h, inner):
            (n, first), (m, second) = term(start + 2 * h), term(start + 2 * h + 1)
            sums[n] += first
            sums[m] += second
            return inner

        lax.fori_loop(0, half, two, 0)

        @pl.when(start + 2 * half < stop)
        def _():
            n, first = term(stop - 1)
            sums[n] += first

        def put(n, inner):

            @pl.when(touched[n] == 1)
            def _():
                buf[n] = sums[n].astype(jnp.bfloat16)
                write(n).start()

            return inner

        return lax.fori_loop(2 * g * KEPT, 2 * (g + 1) * KEPT, put, carry)

    lax.fori_loop(0, ROWS // 2, finish, 0)
    pltpu.make_async_copy(buf, out, out_sem).wait()


def per_device(x_blocks, x_cols, out_cols, branch_flag):
    anywhere = pl.BlockSpec(memory_space=pl.ANY)
    scalars = pl.BlockSpec(memory_space=pltpu.SMEM)
    cols, kept = x_cols.T, out_cols.T
    blocks = x_blocks.reshape(ROWS * SLOTS * PER, PART, BLK)
    shapes = (
        jax.ShapeDtypeStruct((8, TILE, PART, BLK), jnp.bfloat16),
        jax.ShapeDtypeStruct((16, TILE, PART, BLK), jnp.bfloat16),
        jax.ShapeDtypeStruct((24, 1, LANES), jnp.int32),
    )
    ga, gb, meta, share, part, draft = pl.pallas_call(
        gather_kernel,
        name="gather",
        out_shape=shapes + (
            jax.ShapeDtypeStruct((128, 1, LANES), jnp.float32),
            jax.ShapeDtypeStruct((ROWS * KEPT, BLK, BLK), jnp.float32),
            jax.ShapeDtypeStruct((ROWS * KEPT, BLK, BLK), jnp.bfloat16),
        ),
        in_specs=[scalars] * 3 + [anywhere],
        out_specs=[anywhere] * 6,
        scratch_shapes=[
            pltpu.VMEM((TILE, PART, BLK), jnp.bfloat16),
            pltpu.VMEM((TILE, PART, BLK), jnp.bfloat16),
            pltpu.VMEM((2 * TILE + PER, PART, BLK), jnp.bfloat16),
            pltpu.VMEM((2 * TILE + PER, PART, BLK), jnp.bfloat16),
            pltpu.VMEM((ROWS * SLOTS * PER, PART, BLK), jnp.bfloat16),
            pltpu.VMEM((TILE, PART, BLK), jnp.bfloat16),
            pltpu.VMEM((1, LANES), jnp.int32),
            pltpu.VMEM((ROWS * KEPT, BLK, BLK), jnp.float32),
            pltpu.VMEM((ROWS * KEPT, BLK, BLK), jnp.bfloat16),
            pltpu.SMEM((24, 1, LANES), jnp.int32),
            pltpu.VMEM((1, LANES), jnp.float32),
            pltpu.VMEM((8, BLK), jnp.float32),
            pltpu.SemaphoreType.DMA((len(ORDER),)),
            pltpu.SemaphoreType.DMA((len(ORDER),)),
            pltpu.SemaphoreType.DMA((3, 3)),
            pltpu.SemaphoreType.DMA((ROWS // GROUP, 2)),
        ],
        compiler_params=pltpu.CompilerParams(collective_id=0, has_side_effects=True),
    )(kept, cols, branch_flag, blocks)
    purified, trace = pl.pallas_call(
        product_kernel,
        name="product",
        out_shape=(
            jax.ShapeDtypeStruct((ROWS * KEPT, BLK, BLK), jnp.bfloat16),
            jax.ShapeDtypeStruct((1, 1), jnp.float32),
        ),
        in_specs=[scalars] * 3 + [pl.BlockSpec(memory_space=pltpu.VMEM)] + [anywhere] * 4,
        out_specs=[anywhere, scalars],
        scratch_shapes=[
            pltpu.VMEM((ROWS * SLOTS, PER, PART, BLK), jnp.bfloat16),
            pltpu.VMEM((ROWS * SLOTS * SLOTS, PER, PART, BLK), jnp.bfloat16),
            pltpu.VMEM((ROWS * KEPT, BLK, BLK), jnp.float32),
            pltpu.VMEM((ROWS * KEPT, BLK, BLK), jnp.bfloat16),
            pltpu.SMEM((ROWS * KEPT,), jnp.int32),
            pltpu.SMEM((ROWS * SLOTS * SLOTS,), jnp.int32),
            pltpu.SMEM((ROWS * SLOTS * SLOTS,), jnp.int32),
            pltpu.SMEM((ROWS, 4), jnp.int32),
            pltpu.SemaphoreType.DMA((ROWS,)),
            pltpu.SemaphoreType.DMA((ROWS, 2)),
            pltpu.SemaphoreType.DMA,
        ],
    )(meta, kept, branch_flag, share, draft, part, ga, gb)
    return purified.reshape(ROWS, KEPT, BLK, BLK), trace.reshape(1)


def solution(mesh):
    in_specs = (P("row", "col", None, None), P("row", "col"), P("row", "col"), P("row"))
    out_specs = (P("row", "col", None, None), P())
    return jax.shard_map(
        per_device, mesh=mesh, in_specs=in_specs, out_specs=out_specs, check_vma=False
    )
```
